32 devices in a mesh: groups: 2 (over y), tok: 16 (over z, x, core).
Axes of the slice: x: 2, y: 2, z: 4, core: 2. Of those that a mesh axis runs over, the one named last changes fastest.
Arguments:
- query_rows: bfloat16 [8192, 768], P(('groups', 'tok')), parts along dimension 0, may hold values from -6 to 6
- key_rows: bfloat16 [8192, 768], P(('groups', 'tok')), parts along dimension 0, may hold values from -6 to 6
- value_rows: bfloat16 [8192, 768], P(('groups', 'tok')), parts along dimension 0, may hold values from -6 to 6
- out_rows: bfloat16 [8192, 768], P(('groups', 'tok')), parts along dimension 0, may hold values from -6 to 6
- grad_out: bfloat16 [8192, 768], P(('groups', 'tok')), parts along dimension 0, may hold values from -6 to 6
- normalizer: float32 [16, 8192], P(None, ('groups', 'tok')), parts along dimension 1, may hold values from 3 to 5
- keep_tasks: int32 [32, 5], P('groups'), parts along dimension 0, may hold values from 0 to 1, as said below
Outputs:
- grad_query: bfloat16 [8192, 768], P(('groups', 'tok')), parts along dimension 0
- grad_key: bfloat16 [8192, 768], P(('groups', 'tok')), parts along dimension 0
- grad_value: bfloat16 [8192, 768], P(('groups', 'tok')), parts along dimension 0
The draws below stay inside these ranges and needn't reach their ends.
There are 2 independent parts, one for each index of `groups`. The reference program is written for one: setup_inputs(seed, part) draws one part's arguments, and reference() takes and returns one part's arrays. A program takes and returns all parts, laid end to end along the dimension named above; each array names one. Nothing has to cross between parts.
Inputs may be any that keep to these rules, and one draw needn't show every extreme that they name: keep_tasks[a, 2] = 1 for every block a; entries naming a key block outside 0 to 15 are ignored.
All inputs are finite; a program needn't handle non-finite values.
Results may differ from the reference program's by a relative error of at most 0.0053.
Values may be sent and summed in bfloat16 or wider, within the bound.
A program may use at most 128 MiB of HBM per device.

```python
import jax
import jax.numpy as jnp
from jax import lax

D = 768
HEADS = 16
BLOCK = 256
RADIUS = 2
WIN = 5
NBLK = 16
TOKENS = 4096


def draw_keep_tasks(key, part):
    first = jax.random.fold_in(key, 11)
    second = jax.random.fold_in(key, 23)
    density = jax.random.randint(first, (NBLK, 1), 0, 5)
    levels = jax.random.randint(second, (NBLK, WIN), 0, 4)
    column = jnp.arange(WIN)[None, :]
    keep = (levels < density) | (column == RADIUS)
    return jnp.where(keep, 1, 0).astype(jnp.int32)


def steps_of(own_key, dims, pieces, smallest, top_value):
    def one(axis_at, parts):
        heights = jax.random.uniform(jax.random.fold_in(jax.random.fold_in(own_key, 6), axis_at), (parts,), jnp.float32, smallest / len(pieces), top_value / len(pieces))
        return jnp.repeat(jnp.exp(heights), dims[axis_at] // parts).reshape((-1,) + (1,) * (len(dims) - axis_at - 1))

    gain = one(*pieces[0])
    for cut in pieces[1:]:
        gain = gain * one(*cut)
    return gain


def centred(rng, extent, spread, bound, shards=(), held_as=jnp.bfloat16):
    array = jax.random.normal(rng, extent, jnp.float32) * spread
    if len(shards) > 0:
        array = steps_of(rng, extent, shards, -0.22, 0.18) * array
    return jnp.clip(array, min=-bound, max=bound).astype(held_as)


def setup_inputs(seed: int = 0, part: int = 0) -> dict:
    key_list = jax.random.split(jax.random.key(seed), 8)
    own_keys = jax.random.split(jax.random.fold_in(key_list[7], part), 8)
    query_rows = centred(own_keys[0], (TOKENS, D), 1.0, 6.0, ((0, 16),))
    key_rows = centred(own_keys[1], (TOKENS, D), 1.0, 6.0, ((0, 16),))
    value_rows = centred(own_keys[2], (TOKENS, D), 1.0, 6.0, ((0, 16),))
    out_rows = centred(own_keys[3], (TOKENS, D), 1.0, 6.0, ((0, 16),))
    grad_out = centred(own_keys[4], (TOKENS, D), 1.0, 6.0, ((0, 16),))
    normalizer = jnp.clip(3.0 + 2.0 * jax.random.uniform(own_keys[5], (HEADS, TOKENS), jnp.float32) ** steps_of(own_keys[5], (HEADS, TOKENS), ((1, 16),), -0.2, 0.2), 3.0, 5.0)
    keep_tasks = draw_keep_tasks(jax.random.fold_in(jax.random.fold_in(key_list[7], part), 71), part)
    return dict(query_rows=query_rows, key_rows=key_rows, value_rows=value_rows, out_rows=out_rows, grad_out=grad_out, normalizer=normalizer, keep_tasks=keep_tasks)


def task_grads(q_block, dout_block, lse_block, delta_block, k_block, v_block, scale):
    scores = jnp.einsum('qhe,khe->hqk', q_block, k_block) * scale
    probs = jnp.exp(scores - lse_block[:, :, None])
    prob_grad = jnp.einsum('qhe,khe->hqk', dout_block, v_block)
    score_grad = lax.optimization_barrier((probs * (prob_grad - delta_block[:, :, None])).astype(jnp.bfloat16)).astype(jnp.float32)
    probs_low = lax.optimization_barrier(probs.astype(jnp.bfloat16)).astype(jnp.float32)
    term_q = jnp.einsum('hqk,khe->qhe', score_grad, k_block) * scale
    term_k = jnp.einsum('hqk,qhe->khe', score_grad, q_block) * scale
    term_v = jnp.einsum('hqk,qhe->khe', probs_low, dout_block)
    return term_q, term_k, term_v


def reference(query_rows, key_rows, value_rows, out_rows, grad_out, normalizer, keep_tasks):
    width = query_rows.shape[1]
    head_dim = width // HEADS
    scale = head_dim ** -0.5
    shape4 = (NBLK, BLOCK, HEADS, head_dim)
    q_all = query_rows.astype(jnp.float32).reshape(shape4)
    k_all = key_rows.astype(jnp.float32).reshape(shape4)
    v_all = value_rows.astype(jnp.float32).reshape(shape4)
    o_all = out_rows.astype(jnp.float32).reshape(shape4)
    g_all = grad_out.astype(jnp.float32).reshape(shape4)
    delta = jnp.transpose(jnp.sum(g_all * o_all, axis=3), (0, 2, 1))
    lse_all = jnp.transpose(normalizer.astype(jnp.float32).reshape(HEADS, NBLK, BLOCK), (1, 0, 2))
    padding = jnp.zeros((RADIUS, BLOCK, HEADS, head_dim), jnp.float32)
    k_pad = jnp.concatenate([padding, k_all, padding], axis=0)
    v_pad = jnp.concatenate([padding, v_all, padding], axis=0)
    zeros3 = jnp.zeros((BLOCK, HEADS, head_dim), jnp.float32)

    def step(carry, block):
        dk_pad, dv_pad = carry
        q_block = lax.dynamic_index_in_dim(q_all, block, 0, keepdims=False)
        g_block = lax.dynamic_index_in_dim(g_all, block, 0, keepdims=False)
        lse_block = lax.dynamic_index_in_dim(lse_all, block, 0, keepdims=False)
        d_block = lax.dynamic_index_in_dim(delta, block, 0, keepdims=False)
        dq = zeros3
        for j in range(WIN):
            target = block - RADIUS + j
            inside = (target >= 0) & (target < NBLK)
            flag = jnp.where(inside, keep_tasks[block, j], 0)
            slot = (block + j).astype(jnp.int32)
            k_block = lax.dynamic_index_in_dim(k_pad, slot, 0, keepdims=False)
            v_block = lax.dynamic_index_in_dim(v_pad, slot, 0, keepdims=False)

            def live(unused):
                return task_grads(q_block, g_block, lse_block, d_block, k_block, v_block, scale)

            def dead(unused):
                return zeros3, zeros3, zeros3

            term_q, term_k, term_v = lax.cond(flag > 0, live, dead, 0)
            dq = dq + term_q
            old_k = lax.dynamic_index_in_dim(dk_pad, slot, 0, keepdims=False)
            dk_pad = lax.dynamic_update_index_in_dim(dk_pad, old_k + term_k, slot, 0)
            old_v = lax.dynamic_index_in_dim(dv_pad, slot, 0, keepdims=False)
            dv_pad = lax.dynamic_update_index_in_dim(dv_pad, old_v + term_v, slot, 0)
        return (dk_pad, dv_pad), dq

    start = (jnp.zeros_like(k_pad), jnp.zeros_like(v_pad))
    (dk_pad, dv_pad), dq_all = lax.scan(step, start, jnp.arange(NBLK, dtype=jnp.int32))
    total = NBLK * BLOCK
    grad_query = dq_all.reshape(total, width).astype(jnp.bfloat16)
    grad_key = dk_pad[RADIUS:RADIUS + NBLK].reshape(total, width).astype(jnp.bfloat16)
    grad_value = dv_pad[RADIUS:RADIUS + NBLK].reshape(total, width).astype(jnp.bfloat16)
    return grad_query, grad_key, grad_value
```

```python
import functools

import jax
import jax.numpy as jnp
from jax import lax
from jax.experimental import pallas as pl
from jax.experimental.pallas import tpu as pltpu
from jax.sharding import PartitionSpec as P

HEADS = 16
HALF = HEADS // 2
LANES = 128
LOG2E = 1.4426950408889634
MESH = pl.DeviceIdType.MESH
F32 = jnp.float32
BF16 = jnp.bfloat16
AHEAD = 2
HOLD = 5


def dot_nn(a, b):
    return lax.dot_general(a, b, (((1,), (0,)), ((), ())), preferred_element_type=F32)


def dot_nt(a, b):
    return lax.dot_general(a, b, (((1,), (1,)), ((), ())), preferred_element_type=F32)


def kernel(
    count, q_hbm, k_hbm, v_hbm, o_hbm, g_hbm, lse_ref, keep_ref,
    dq_out, dk_out, dv_out,
    q_in, k_in, v_in, o_in, g_in,
    qbuf, qaway, kbuf, kaway, sbuf, saway, dqx, dqo, dkv,
    zout, zback, xout, xback, own, mine, theirs,
    ins, xs, xr, xss, xsr, ms, mr, ks, kr, mss, msr, zs, zr, zss, zsr, bs, br, rs, rr, fs, fr,
):
    tok = lax.axis_index("tok")
    core, chip = tok % 2, tok // 2
    side, plane = chip % 2, chip // 2
    planes = count // 4
    other = 1 - core
    mate = tok + 1 - 2 * core
    across = 2 * (chip + 1 - 2 * side)
    step = 4 * (1 - 2 * side)
    fwd, src = tok + step, tok - step
    has_low, has_high = plane > 0, plane < planes - 1
    has_fwd = jnp.logical_or(jnp.logical_and(side == 0, has_high), jnp.logical_and(side == 1, has_low))
    has_src = jnp.logical_or(jnp.logical_and(side == 0, has_low), jnp.logical_and(side == 1, has_high))
    xslot = 4 * (1 - side)
    zslot = 4 * side
    width = q_in.shape[1]
    dim = width // HEADS
    half_width = width // 2
    scale = dim ** -0.5

    def load(i, src_ref, dst_ref):
        return pltpu.make_async_copy(src_ref, dst_ref, ins.at[i])

    loads = [load(0, q_hbm, q_in), load(1, g_hbm, g_in), load(2, o_hbm, o_in), load(3, k_hbm, k_in), load(4, v_hbm, v_in)]
    for copy in loads:
        copy.start()

    barrier = pltpu.get_barrier_semaphore()

    def greet(target):
        pl.semaphore_signal(barrier, inc=1, device_id={"tok": target}, device_id_type=MESH)

    greet(mate)
    greet(across)
    greet(across + 1)

    @pl.when(has_fwd)
    def _():
        greet(fwd)

    @pl.when(has_src)
    def _():
        greet(src)

    def remote(src_ref, dst_ref, send, recv, target):
        return pltpu.make_async_remote_copy(
            src_ref=src_ref, dst_ref=dst_ref, send_sem=send, recv_sem=recv,
            device_id={"tok": target}, device_id_type=MESH,
        )

    def x_near(j):
        return remote(qbuf.at[2 + core, j], qbuf.at[zslot + core, j], xs.at[0, j], xr.at[0, j], across + core)

    def x_cross(j):
        return remote(qaway.at[j], qbuf.at[zslot + core, j], xs.at[1, j], xr.at[1, j], across + other)

    def x_stat(i):
        return remote(sbuf.at[2 + core] if i == 0 else saway, sbuf.at[zslot + core], xss.at[i], xsr.at[i],
                      across + (core if i == 0 else other))

    def x_in(i, j):
        parity = core if i == 0 else other
        return remote(qaway.at[0], qbuf.at[xslot + parity, j], xs.at[i, j], xr.at[i, j], across)

    def x_stat_in(i):
        parity = core if i == 0 else other
        return remote(saway, sbuf.at[xslot + parity], xss.at[i], xsr.at[i], across)

    def m_q(j):
        return remote(qaway.at[j], qbuf.at[2 + core, j], ms.at[j], mr.at[j], mate)

    def m_k(j):
        return remote(kaway.at[j], kbuf.at[core, j], ks.at[j], kr.at[j], mate)

    def m_stat():
        return remote(saway, sbuf.at[2 + core], mss, msr, mate)

    def m_q_in(j):
        return remote(qaway.at[0], qbuf.at[2 + other, j], ms.at[j], mr.at[j], mate)

    def m_k_in(j):
        return remote(kaway.at[0], kbuf.at[other, j], ks.at[j], kr.at[j], mate)

    def m_stat_in():
        return remote(saway, sbuf.at[2 + other], mss, msr, mate)

    def z_q(i, j):
        parity = core if i == 0 else other
        return remote(qbuf.at[xslot + parity, j], qbuf.at[zslot + parity, j], zs.at[i, j], zr.at[i, j], fwd)

    def z_q_in(i, j):
        parity = core if i == 0 else other
        return remote(qbuf.at[zslot + parity, j], qbuf.at[zslot + parity, j], zs.at[i, j], zr.at[i, j], src)

    def z_stat():
        return remote(sbuf.at[pl.ds(xslot, 2)], sbuf.at[pl.ds(zslot, 2)], zss, zsr, fwd)

    def z_stat_in():
        return remote(sbuf.at[pl.ds(zslot, 2)], sbuf.at[pl.ds(zslot, 2)], zss, zsr, src)

    def z_back(j):
        return remote(zout.at[j], zback.at[j], bs.at[j], br.at[j], src)

    def z_back_in(j):
        return remote(zout.at[j], zback.at[j], bs.at[j], br.at[j], fwd)

    def rows(j):
        return pl.ds(pl.multiple_of(j * dim, 16), dim)

    def x_back(i, j):
        return remote(xout.at[i, j], xback.at[core, rows(j)], rs.at[i, j], rr.at[core, j], across + i)

    def x_back_in(i, j):
        return remote(xout.at[0, 0], xback.at[i, rows(j)], rs.at[i, j], rr.at[i, j], across)

    def m_back(j):
        return remote(mine.at[:, rows(j)], theirs.at[:, rows(j)], fs.at[j], fr.at[j], mate)

    def lanes(half, k):
        return pl.ds(pl.multiple_of(half * half_width + k * LANES, LANES), LANES)

    def pieces(k):
        at = k * LANES
        while at < (k + 1) * LANES:
            j = at // dim
            end = min((j + 1) * dim, (k + 1) * LANES)
            yield j, at - j * dim, end - j * dim, at - k * LANES, end - k * LANES
            at = end

    def flip(ref, k, near, far, i):
        for half, put in ((core, near), (other, far)):
            block = ref[:, lanes(half, k)].T
            for j, lo, hi, a, b in pieces(k):
                put(j, i, lo, hi, block[a:b])

    def q_near(j, i, lo, hi, x):
        qbuf[2 + core, j, i, lo:hi] = x

    def q_far(j, i, lo, hi, x):
        qaway[j, i, lo:hi] = x

    def k_near(j, i, lo, hi, x):
        kbuf[core, j, i, lo:hi] = x

    def k_far(j, i, lo, hi, x):
        kaway[j, i, lo:hi] = x

    chunks = half_width // LANES
    ready = 0
    for k in range(chunks):
        if k == 0:
            loads[0].wait()
        flip(q_in, k, q_near, q_far, 0)
        if k == 0:
            loads[1].wait()
        flip(g_in, k, q_near, q_far, 1)
        if k == 0:
            pl.semaphore_wait(barrier, 3 + has_fwd.astype(jnp.int32) + has_src.astype(jnp.int32))
        done = (k + 1) * LANES // dim
        for j in range(ready, done):
            x_near(j).start()
            x_cross(j).start()
        for j in range(ready, done):
            m_q(j).start()
        ready = done
        if k == 0:
            loads[2].wait()
            head = lax.broadcasted_iota(jnp.int32, (HEADS, width), 0) * dim
            lane = lax.broadcasted_iota(jnp.int32, (HEADS, width), 1)
            pick = jnp.where(jnp.logical_and(lane >= head, lane < head + dim), 1.0, 0.0).astype(BF16)
            prod = g_in[...].astype(F32) * o_in[...].astype(F32)
            high = prod.astype(BF16)
            low = (prod - high.astype(F32)).astype(BF16)
            delta = dot_nt(pick, high) + dot_nt(pick, low)
            lse2 = lse_ref[...] * LOG2E
            first = core == 0
            sbuf[2 + core, 0] = jnp.where(first, lse2[:HALF], lse2[HALF:])
            sbuf[2 + core, 1] = jnp.where(first, delta[:HALF], delta[HALF:])
            saway[0] = jnp.where(first, lse2[HALF:], lse2[:HALF])
            saway[1] = jnp.where(first, delta[HALF:], delta[:HALF])
            x_stat(0).start()
            x_stat(1).start()
            m_stat().start()

    loads[3].wait()
    loads[4].wait()
    ready = 0
    for k in range(chunks):
        flip(k_in, k, k_near, k_far, 0)
        flip(v_in, k, k_near, k_far, 1)
        done = (k + 1) * LANES // dim
        for j in range(ready, done):
            m_k(j).start()
        ready = done

    @pl.when(jnp.logical_not(has_fwd))
    def _():
        zback[...] = jnp.zeros(zback.shape, BF16)

    first_block = plane * 4 + side * 2

    def task(c, slot, j, keys, values):
        block = first_block + slot - 2
        flag = keep_ref[c + 4 - slot, block]
        gone = (1 - flag).astype(F32) * 1e30
        q_t, g_t = qbuf[slot, j, 0], qbuf[slot, j, 1]
        lse = sbuf[slot, 0, pl.ds(j, 1), :] + gone
        delta = sbuf[slot, 1, pl.ds(j, 1), :]
        probs = jnp.exp2(dot_nn(keys, q_t) * (scale * LOG2E) - lse)
        grad = (probs * (dot_nn(values, g_t) - delta)).astype(BF16)
        return q_t, g_t, grad, probs.astype(BF16)

    def run(j, work, fresh):
        found = {}
        for c, slots in work:
            keys_t = kbuf[c, j, 0]
            keys = keys_t.T
            values = kbuf[c, j, 1].T
            parts = [task(c, slot, j, keys, values) for slot, _ in slots]
            q_all, g_all, grads, lows = [jnp.concatenate([p[i] for p in parts], axis=1) for i in range(4)]
            dk, dv = dot_nt(q_all, grads), dot_nt(g_all, lows)
            for (_, name), p in zip(slots, parts):
                found.setdefault(name, []).append((keys_t, p[2]))
            if fresh:
                dkv[j, c, 0] = dk
                dkv[j, c, 1] = dv
            else:
                dkv[j, c, 0] += dk
                dkv[j, c, 1] += dv
        return {
            name: dot_nn(
                jnp.concatenate([t[0] for t in terms], axis=1),
                jnp.concatenate([t[1] for t in terms], axis=0),
            )
            for name, terms in found.items()
        }

    def inner(j):
        m_q_in(j).wait_recv()
        m_k_in(j).wait_recv()

        @pl.when(j == 0)
        def _():
            m_stat_in().wait_recv()

        got = run(j, ((0, ((2, 0), (3, 1))), (1, ((2, 0), (3, 1)))), True)
        dqo[0, j] = got[0]
        dqo[1, j] = got[1]

    def x_get(j):
        for i in range(2):
            x_in(i, j).wait_recv()

            @pl.when(has_fwd)
            def _():
                z_q(i, j).start()

        @pl.when(j == 0)
        def _():
            x_stat_in(0).wait_recv()
            x_stat_in(1).wait_recv()

            @pl.when(has_fwd)
            def _():
                z_stat().start()

    def x_run(j):
        near, far, close = side, 1 - side, 1 - side
        got = run(j, ((close, ((xslot + near, 0), (xslot + far, 1))), (1 - close, ((xslot + near, 0),))), False)
        dqx[j, near] = got[0]
        dqx[j, far] = got[1]

    def z_run(j):
        z_q_in(0, j).wait_recv()
        z_q_in(1, j).wait_recv()

        @pl.when(j == 0)
        def _():
            z_stat_in().wait_recv()

        near, far, close = 1 - side, side, side
        got = run(j, ((close, ((zslot + near, 0), (zslot + far, 1))), (1 - close, ((zslot + near, 0),))), False)
        zout[j, near] = (got[0] * scale).astype(BF16)
        zout[j, far] = (got[1] * scale).astype(BF16)
        z_back(j).start()

    def x_ret(j):
        @pl.when(has_fwd)
        def _():
            z_back_in(j).wait_recv()

        for i in range(2):
            xout[i, j] = (dqx[j, i] * scale + zback[j, i].astype(F32)).astype(BF16)
            x_back(i, j).start()

    def share(j):
        mine[0, rows(j)] = (dqo[other, j] * scale).astype(BF16)
        mine[1, rows(j)] = (dkv[j, other, 0] * scale).astype(BF16)
        mine[2, rows(j)] = dkv[j, other, 1].astype(BF16)
        m_back(j).start()
        own[0, rows(j)] = (dkv[j, core, 0] * scale).astype(BF16)
        own[1, rows(j)] = dkv[j, core, 1].astype(BF16)

    for j in range(AHEAD):
        inner(j)

    @pl.loop(0, HALF + 1)
    def _(i):
        @pl.when(i < HALF)
        def _():
            x_get(i)
            x_run(i)

        @pl.when(i + AHEAD < HALF)
        def _():
            inner(i + AHEAD)

        @pl.when(i > 0)
        def _():
            @pl.when(has_src)
            def _():
                z_run(i - 1)

            share(i - 1)

        @pl.when(i >= HOLD)
        def _():
            for r in range(2):
                x_ret(2 * (i - HOLD) + r)

    for j in range(2 * (HALF + 1 - HOLD), HALF):
        x_ret(j)

    def put(out, half, k, x):
        out[:, lanes(half, k)] = x.T

    for j in range(HALF):
        m_back(j).wait_recv()
    for k in range(chunks):
        part = pl.ds(k * LANES, LANES)
        put(dk_out, core, k, own[0, part])
        put(dk_out, other, k, theirs[1, part])
        put(dv_out, core, k, own[1, part])
        put(dv_out, other, k, theirs[2, part])

    ready = 0
    for k in range(chunks):
        done = -(-(k + 1) * LANES // dim)
        for j in range(ready, done):
            x_back_in(0, j).wait_recv()
            x_back_in(1, j).wait_recv()
            own[0, rows(j)] = (dqo[core, j] * scale + xback[core, rows(j)].astype(F32)).astype(BF16)
        ready = done
        part = pl.ds(k * LANES, LANES)
        put(dq_out, core, k, own[0, part])
        put(dq_out, other, k, (theirs[0, part].astype(F32) + xback[other, part].astype(F32)).astype(BF16))

    for i in range(2):
        x_stat(i).wait_send()
    m_stat().wait_send()

    @pl.when(has_fwd)
    def _():
        z_stat().wait_send()

    @pl.loop(0, HALF)
    def _(j):
        x_near(j).wait_send()
        x_cross(j).wait_send()
        m_q(j).wait_send()
        m_k(j).wait_send()
        m_back(j).wait_send()
        x_back(0, j).wait_send()
        x_back(1, j).wait_send()

        @pl.when(has_fwd)
        def _():
            z_q(0, j).wait_send()
            z_q(1, j).wait_send()

        @pl.when(has_src)
        def _():
            z_back(j).wait_send()


def store(*refs):
    for i in range(3):
        refs[3 + i][...] = refs[i][...]


def per_device(count, query_rows, key_rows, value_rows, out_rows, grad_out, normalizer, keep_tasks):
    block, width = query_rows.shape
    dim = width // HEADS
    half = width // 2
    vmem = pl.BlockSpec(memory_space=pltpu.VMEM)
    hbm = pl.BlockSpec(memory_space=pl.ANY)
    dma = pltpu.SemaphoreType.DMA
    outs = [jax.ShapeDtypeStruct((block, width), BF16)] * 3
    packed = pl.pallas_call(
        functools.partial(kernel, count),
        out_shape=outs,
        in_specs=[hbm] * 5 + [vmem, pl.BlockSpec(memory_space=pltpu.SMEM)],
        out_specs=[vmem] * 3,
        scratch_shapes=[
            *[pltpu.VMEM((block, width), BF16)] * 5,
            pltpu.VMEM((6, HALF, 2, dim, block), BF16),
            pltpu.VMEM((HALF, 2, dim, block), BF16),
            pltpu.VMEM((2, HALF, 2, dim, block), BF16),
            pltpu.VMEM((HALF, 2, dim, block), BF16),
            pltpu.VMEM((6, 2, HALF, block), F32),
            pltpu.VMEM((2, HALF, block), F32),
            pltpu.VMEM((HALF, 2, dim, block), F32),
            pltpu.VMEM((2, HALF, dim, block), F32),
            pltpu.VMEM((HALF, 2, 2, dim, block), F32),
            pltpu.VMEM((HALF, 2, dim, block), BF16),
            pltpu.VMEM((HALF, 2, dim, block), BF16),
            pltpu.VMEM((2, HALF, dim, block), BF16),
            pltpu.VMEM((2, half, block), BF16),
            pltpu.VMEM((2, half, block), BF16),
            pltpu.VMEM((3, half, block), BF16),
            pltpu.VMEM((3, half, block), BF16),
            dma((5,)),
            dma((2, HALF)), dma((2, HALF)), dma((2,)), dma((2,)),
            dma((HALF,)), dma((HALF,)), dma((HALF,)), dma((HALF,)), dma, dma,
            dma((2, HALF)), dma((2, HALF)), dma, dma,
            dma((HALF,)), dma((HALF,)),
            dma((2, HALF)), dma((2, HALF)),
            dma((HALF,)), dma((HALF,)),
        ],
        compiler_params=pltpu.CompilerParams(
            collective_id=0, has_side_effects=True, vmem_limit_bytes=60 * 1024 * 1024
        ),
    )(query_rows, key_rows, value_rows, out_rows, grad_out, normalizer, keep_tasks.T)
    return pl.pallas_call(
        store,
        out_shape=outs,
        in_specs=[vmem] * 3,
        out_specs=[vmem] * 3,
    )(*packed)


def solution(mesh):
    rows = P(("groups", "tok"), None)
    return jax.shard_map(
        functools.partial(per_device, mesh.shape["tok"]),
        mesh=mesh,
        in_specs=(rows,) * 5 + (P(None, ("groups", "tok")), P("groups", None)),
        out_specs=(rows,) * 3,
        check_vma=False,
    )
```

```python
import functools

import jax
import jax.numpy as jnp
from jax import lax
from jax.experimental import pallas as pl
from jax.experimental.pallas import tpu as pltpu
from jax.sharding import PartitionSpec as P

HEADS = 16
HALF = HEADS // 2
LANES = 128
LOG2E = 1.4426950408889634
MESH = pl.DeviceIdType.MESH
F32 = jnp.float32
BF16 = jnp.bfloat16
AHEAD = 2
LAG = 3


def dot_nn(a, b):
    return lax.dot_general(a, b, (((1,), (0,)), ((), ())), preferred_element_type=F32)


def dot_nt(a, b):
    return lax.dot_general(a, b, (((1,), (1,)), ((), ())), preferred_element_type=F32)


def kernel(
    count, q_hbm, k_hbm, v_hbm, o_hbm, g_hbm, lse_ref, keep_ref,
    dq_out, dk_out, dv_out,
    q_in, k_in, v_in, o_in, g_in,
    qbuf, qaway, kbuf, kaway, sbuf, saway, dqo, dkv,
    zout, zback, xout, xback, own, mine, theirs,
    ins, xs, xr, xss, xsr, ms, mr, ks, kr, mss, msr, zs, zr, bs, br, rs, rr, fs, fr,
):
    tok = lax.axis_index("tok")
    core, chip = tok % 2, tok // 2
    side, plane = chip % 2, chip // 2
    planes = count // 4
    other = 1 - core
    mate = tok + 1 - 2 * core
    across = 2 * (chip + 1 - 2 * side)
    step = 4 * (1 - 2 * side)
    fwd, src = tok + step, tok - step
    has_low, has_high = plane > 0, plane < planes - 1
    has_fwd = jnp.logical_or(jnp.logical_and(side == 0, has_high), jnp.logical_and(side == 1, has_low))
    has_src = jnp.logical_or(jnp.logical_and(side == 0, has_low), jnp.logical_and(side == 1, has_high))
    width = q_in.shape[1]
    dim = width // HEADS
    half_width = width // 2
    scale = dim ** -0.5

    def load(i, src_ref, dst_ref):
        return pltpu.make_async_copy(src_ref, dst_ref, ins.at[i])

    loads = [load(0, q_hbm, q_in), load(1, g_hbm, g_in), load(2, o_hbm, o_in), load(3, k_hbm, k_in), load(4, v_hbm, v_in)]
    for copy in loads:
        copy.start()

    barrier = pltpu.get_barrier_semaphore()

    def greet(target):
        pl.semaphore_signal(barrier, inc=1, device_id={"tok": target}, device_id_type=MESH)

    greet(mate)
    greet(across)
    greet(across + 1)

    @pl.when(has_fwd)
    def _():
        greet(fwd)
        greet(fwd + other - core)

    @pl.when(has_src)
    def _():
        greet(src)
        greet(src + other - core)

    def remote(src_ref, dst_ref, send, recv, target):
        return pltpu.make_async_remote_copy(
            src_ref=src_ref, dst_ref=dst_ref, send_sem=send, recv_sem=recv,
            device_id={"tok": target}, device_id_type=MESH,
        )

    def x_near(j):
        return remote(qbuf.at[core, j], qbuf.at[2 + core, j], xs.at[0, j], xr.at[0, j], across + core)

    def x_cross(j):
        return remote(qaway.at[j], qbuf.at[2 + core, j], xs.at[1, j], xr.at[1, j], across + other)

    def x_stat(i):
        return remote(sbuf.at[core] if i == 0 else saway, sbuf.at[2 + core], xss.at[i], xsr.at[i],
                      across + (core if i == 0 else other))

    def x_in(i, j):
        parity = core if i == 0 else other
        return remote(qaway.at[0], qbuf.at[2 + parity, j], xs.at[i, j], xr.at[i, j], across)

    def x_stat_in(i):
        parity = core if i == 0 else other
        return remote(saway, sbuf.at[2 + parity], xss.at[i], xsr.at[i], across)

    def m_q(j):
        return remote(qaway.at[j], qbuf.at[core, j], ms.at[j], mr.at[j], mate)

    def m_k(j):
        return remote(kaway.at[j], kbuf.at[core, j], ks.at[j], kr.at[j], mate)

    def m_stat():
        return remote(saway, sbuf.at[core], mss, msr, mate)

    def m_q_in(j):
        return remote(qaway.at[0], qbuf.at[other, j], ms.at[j], mr.at[j], mate)

    def m_k_in(j):
        return remote(kaway.at[0], kbuf.at[other, j], ks.at[j], kr.at[j], mate)

    def m_stat_in():
        return remote(saway, sbuf.at[other], mss, msr, mate)

    def z_k(i, j):
        return remote(kbuf.at[core, j] if i == 0 else kaway.at[j], kbuf.at[2 + core, j],
                      zs.at[i, j], zr.at[i, j], src + (0 if i == 0 else other - core))

    def z_k_in(i, j):
        parity = core if i == 0 else other
        return remote(kaway.at[0], kbuf.at[2 + parity, j], zs.at[i, j], zr.at[i, j], fwd)

    def z_back(j):
        return remote(zout.at[j], zback.at[j], bs.at[j], br.at[j], fwd)

    def z_back_in(j):
        return remote(zout.at[j], zback.at[j], bs.at[j], br.at[j], src)

    def rows(j):
        return pl.ds(pl.multiple_of(j * dim, 16), dim)

    def x_back(i, j):
        return remote(xout.at[i, j], xback.at[core, rows(j)], rs.at[i, j], rr.at[core, j], across + i)

    def x_back_in(i, j):
        return remote(xout.at[0, 0], xback.at[i, rows(j)], rs.at[i, j], rr.at[i, j], across)

    def m_back(j):
        return remote(mine.at[:, rows(j)], theirs.at[:, rows(j)], fs.at[j], fr.at[j], mate)

    def lanes(half, k):
        return pl.ds(pl.multiple_of(half * half_width + k * LANES, LANES), LANES)

    def pieces(k):
        at = k * LANES
        while at < (k + 1) * LANES:
            j = at // dim
            end = min((j + 1) * dim, (k + 1) * LANES)
            yield j, at - j * dim, end - j * dim, at - k * LANES, end - k * LANES
            at = end

    def flip(ref, k, near, far, i):
        for half, put in ((core, near), (other, far)):
            block = ref[:, lanes(half, k)].T
            for j, lo, hi, a, b in pieces(k):
                put(j, i, lo, hi, block[a:b])

    def q_near(j, i, lo, hi, x):
        qbuf[core, j, i, lo:hi] = x

    def q_far(j, i, lo, hi, x):
        qaway[j, i, lo:hi] = x

    def k_near(j, i, lo, hi, x):
        kbuf[core, j, i, lo:hi] = x

    def k_far(j, i, lo, hi, x):
        kaway[j, i, lo:hi] = x

    chunks = half_width // LANES
    ready = 0
    for k in range(chunks):
        if k == 0:
            loads[0].wait()
        flip(q_in, k, q_near, q_far, 0)
        if k == 0:
            loads[1].wait()
        flip(g_in, k, q_near, q_far, 1)
        if k == 0:
            pl.semaphore_wait(barrier, 3 + 2 * has_fwd.astype(jnp.int32) + 2 * has_src.astype(jnp.int32))
        done = (k + 1) * LANES // dim
        for j in range(ready, done):
            x_near(j).start()
            x_cross(j).start()
        for j in range(ready, done):
            m_q(j).start()
        ready = done
        if k == 0:
            loads[2].wait()
            head = lax.broadcasted_iota(jnp.int32, (HEADS, width), 0) * dim
            lane = lax.broadcasted_iota(jnp.int32, (HEADS, width), 1)
            pick = jnp.where(jnp.logical_and(lane >= head, lane < head + dim), 1.0, 0.0).astype(BF16)
            prod = g_in[...].astype(F32) * o_in[...].astype(F32)
            high = prod.astype(BF16)
            low = (prod - high.astype(F32)).astype(BF16)
            delta = dot_nt(pick, high) + dot_nt(pick, low)
            lse2 = lse_ref[...] * LOG2E
            first = core == 0
            sbuf[core, 0] = jnp.where(first, lse2[:HALF], lse2[HALF:])
            sbuf[core, 1] = jnp.where(first, delta[:HALF], delta[HALF:])
            saway[0] = jnp.where(first, lse2[HALF:], lse2[:HALF])
            saway[1] = jnp.where(first, delta[HALF:], delta[:HALF])
            x_stat(0).start()
            x_stat(1).start()
            m_stat().start()

    loads[3].wait()
    loads[4].wait()
    ready = 0
    for k in range(chunks):
        flip(k_in, k, k_near, k_far, 0)
        flip(v_in, k, k_near, k_far, 1)
        done = (k + 1) * LANES // dim
        for j in range(ready, done):
            m_k(j).start()

        @pl.when(has_src)
        def _():
            for j in range(ready, done):
                z_k(0, j).start()
                z_k(1, j).start()

        ready = done

    @pl.when(jnp.logical_not(has_src))
    def _():
        zback[...] = jnp.zeros(zback.shape, BF16)

    first_block = plane * 4 + side * 2
    across_block = plane * 4 + (1 - side) * 2

    def task(key, slot, query, j, keys, values):
        flag = keep_ref[key - query + 2, query]
        gone = (1 - flag).astype(F32) * 1e30
        q_t, g_t = qbuf[slot, j, 0], qbuf[slot, j, 1]
        lse = sbuf[slot, 0, pl.ds(j, 1), :] + gone
        delta = sbuf[slot, 1, pl.ds(j, 1), :]
        probs = jnp.exp2(dot_nn(keys, q_t) * (scale * LOG2E) - lse)
        grad = (probs * (dot_nn(values, g_t) - delta)).astype(BF16)
        return q_t, g_t, grad, probs.astype(BF16)

    def run(j, work):
        found, sums = {}, []
        for c, key, slots in work:
            keys_t = kbuf[c, j, 0]
            keys = keys_t.T
            values = kbuf[c, j, 1].T
            parts = [task(key, slot, query, j, keys, values) for slot, query, _ in slots]
            q_all, g_all, grads, lows = [jnp.concatenate([p[i] for p in parts], axis=1) for i in range(4)]
            sums.append((dot_nt(q_all, grads), dot_nt(g_all, lows)))
            for (_, _, name), p in zip(slots, parts):
                found.setdefault(name, []).append((keys_t, p[2]))
        out = {
            name: dot_nn(
                jnp.concatenate([t[0] for t in terms], axis=1),
                jnp.concatenate([t[1] for t in terms], axis=0),
            )
            for name, terms in found.items()
        }
        return out, sums

    def inner(j):
        m_q_in(j).wait_recv()
        m_k_in(j).wait_recv()

        @pl.when(j == 0)
        def _():
            m_stat_in().wait_recv()

        queries = [(b, first_block + b, b) for b in range(2)]
        got, sums = run(j, [(c, first_block + c, queries) for c in range(2)])
        for b in range(2):
            dqo[b, j] = got[b]
            dkv[j, b, 0] = sums[b][0]
            dkv[j, b, 1] = sums[b][1]

    near = (2 + side, across_block + side, 0)
    far = (3 - side, across_block + 1 - side, 1)
    close = 1 - side
    local = [(close, first_block + close, [near, far]), (1 - close, first_block + 1 - close, [near])]
    beyond = [(2 + side, first_block + step + side, [near, far]), (3 - side, first_block + step + 1 - side, [far])]

    def x_run(j):
        x_in(0, j).wait_recv()
        x_in(1, j).wait_recv()

        @pl.when(j == 0)
        def _():
            x_stat_in(0).wait_recv()
            x_stat_in(1).wait_recv()

        def finish(got, sums):
            for i, c in enumerate((close, 1 - close)):
                dkv[j, c, 0] += sums[i][0]
                dkv[j, c, 1] += sums[i][1]
            xout[side, j] = (got[0] * scale).astype(BF16)
            xout[1 - side, j] = (got[1] * scale).astype(BF16)

        @pl.when(has_fwd)
        def _():
            z_k_in(0, j).wait_recv()
            z_k_in(1, j).wait_recv()
            got, sums = run(j, local + beyond)
            finish(got, sums[:2])
            for i, c in enumerate((side, 1 - side)):
                zout[j, c, 0] = (sums[2 + i][0] * scale).astype(BF16)
                zout[j, c, 1] = sums[2 + i][1].astype(BF16)
            z_back(j).start()

        @pl.when(jnp.logical_not(has_fwd))
        def _():
            finish(*run(j, local))

        x_back(0, j).start()
        x_back(1, j).start()

    def share(j):
        @pl.when(has_src)
        def _():
            z_back_in(j).wait_recv()

        def total(c):
            return ((dkv[j, c, 0] * scale + zback[j, c, 0].astype(F32)).astype(BF16),
                    (dkv[j, c, 1] + zback[j, c, 1].astype(F32)).astype(BF16))

        mine[0, rows(j)] = (dqo[other, j] * scale).astype(BF16)
        mine[1, rows(j)], mine[2, rows(j)] = total(other)
        m_back(j).start()
        own[0, rows(j)], own[1, rows(j)] = total(core)

    for j in range(AHEAD):
        inner(j)

    @pl.loop(0, HALF)
    def _(i):
        x_run(i)

        @pl.when(i + AHEAD < HALF)
        def _():
            inner(i + AHEAD)

        @pl.when(i >= LAG)
        def _():
            share(i - LAG)

    for j in range(HALF - LAG, HALF):
        share(j)

    def put(out, half, k, x):
        out[:, lanes(half, k)] = x.T

    for j in range(HALF):
        m_back(j).wait_recv()
    for k in range(chunks):
        part = pl.ds(k * LANES, LANES)
        put(dk_out, core, k, own[0, part])
        put(dk_out, other, k, theirs[1, part])
        put(dv_out, core, k, own[1, part])
        put(dv_out, other, k, theirs[2, part])

    ready = 0
    for k in range(chunks):
        done = -(-(k + 1) * LANES // dim)
        for j in range(ready, done):
            x_back_in(0, j).wait_recv()
            x_back_in(1, j).wait_recv()
            own[0, rows(j)] = (dqo[core, j] * scale + xback[core, rows(j)].astype(F32)).astype(BF16)
        ready = done
        part = pl.ds(k * LANES, LANES)
        put(dq_out, core, k, own[0, part])
        put(dq_out, other, k, (theirs[0, part].astype(F32) + xback[other, part].astype(F32)).astype(BF16))

    for i in range(2):
        x_stat(i).wait_send()
    m_stat().wait_send()

    @pl.loop(0, HALF)
    def _(j):
        x_near(j).wait_send()
        x_cross(j).wait_send()
        m_q(j).wait_send()
        m_k(j).wait_send()
        m_back(j).wait_send()
        x_back(0, j).wait_send()
        x_back(1, j).wait_send()

        @pl.when(has_src)
        def _():
            z_k(0, j).wait_send()
            z_k(1, j).wait_send()

        @pl.when(has_fwd)
        def _():
            z_back(j).wait_send()


def store(*refs):
    for i in range(3):
        refs[3 + i][...] = refs[i][...]


def per_device(count, query_rows, key_rows, value_rows, out_rows, grad_out, normalizer, keep_tasks):
    block, width = query_rows.shape
    dim = width // HEADS
    half = width // 2
    vmem = pl.BlockSpec(memory_space=pltpu.VMEM)
    hbm = pl.BlockSpec(memory_space=pl.ANY)
    dma = pltpu.SemaphoreType.DMA
    outs = [jax.ShapeDtypeStruct((block, width), BF16)] * 3
    packed = pl.pallas_call(
        functools.partial(kernel, count),
        out_shape=outs,
        in_specs=[hbm] * 5 + [vmem, pl.BlockSpec(memory_space=pltpu.SMEM)],
        out_specs=[vmem] * 3,
        scratch_shapes=[
            *[pltpu.VMEM((block, width), BF16)] * 5,
            pltpu.VMEM((4, HALF, 2, dim, block), BF16),
            pltpu.VMEM((HALF, 2, dim, block), BF16),
            pltpu.VMEM((4, HALF, 2, dim, block), BF16),
            pltpu.VMEM((HALF, 2, dim, block), BF16),
            pltpu.VMEM((4, 2, HALF, block), F32),
            pltpu.VMEM((2, HALF, block), F32),
            pltpu.VMEM((2, HALF, dim, block), F32),
            pltpu.VMEM((HALF, 2, 2, dim, block), F32),
            pltpu.VMEM((HALF, 2, 2, dim, block), BF16),
            pltpu.VMEM((HALF, 2, 2, dim, block), BF16),
            pltpu.VMEM((2, HALF, dim, block), BF16),
            pltpu.VMEM((2, half, block), BF16),
            pltpu.VMEM((2, half, block), BF16),
            pltpu.VMEM((3, half, block), BF16),
            pltpu.VMEM((3, half, block), BF16),
            dma((5,)),
            dma((2, HALF)), dma((2, HALF)), dma((2,)), dma((2,)),
            dma((HALF,)), dma((HALF,)), dma((HALF,)), dma((HALF,)), dma, dma,
            dma((2, HALF)), dma((2, HALF)),
            dma((HALF,)), dma((HALF,)),
            dma((2, HALF)), dma((2, HALF)),
            dma((HALF,)), dma((HALF,)),
        ],
        compiler_params=pltpu.CompilerParams(
            collective_id=0, has_side_effects=True, vmem_limit_bytes=60 * 1024 * 1024
        ),
    )(query_rows, key_rows, value_rows, out_rows, grad_out, normalizer, keep_tasks.T)
    return pl.pallas_call(
        store,
        out_shape=outs,
        in_specs=[vmem] * 3,
        out_specs=[vmem] * 3,
    )(*packed)


def solution(mesh):
    rows = P(("groups", "tok"), None)
    return jax.shard_map(
        functools.partial(per_device, mesh.shape["tok"]),
        mesh=mesh,
        in_specs=(rows,) * 5 + (P(None, ("groups", "tok")), P("groups", None)),
        out_specs=(rows,) * 3,
        check_vma=False,
    )
```

```python
import functools

import jax
import jax.numpy as jnp
from jax import lax
from jax.experimental import pallas as pl
from jax.experimental.pallas import tpu as pltpu
from jax.sharding import PartitionSpec as P

HEADS = 16
HALF = HEADS // 2
LANES = 128
LOG2E = 1.4426950408889634
MESH = pl.DeviceIdType.MESH
F32 = jnp.float32
BF16 = jnp.bfloat16
AHEAD = 2
LAG = 3


def dot_nn(a, b):
    return lax.dot_general(a, b, (((1,), (0,)), ((), ())), preferred_element_type=F32)


def dot_nt(a, b):
    return lax.dot_general(a, b, (((1,), (1,)), ((), ())), preferred_element_type=F32)


def kernel(
    count, q_hbm, k_hbm, v_hbm, o_hbm, g_hbm, lse_hbm, keep_hbm,
    dq_out, dk_out, dv_out,
    q_in, k_in, v_in, o_in, g_in, lse_ref, keep_ref,
    qbuf, qaway, kbuf, kaway, sbuf, saway, dqo, dkv,
    zout, zback, xout, xback, own, mine, theirs,
    ins, xs, xr, xss, xsr, ms, mr, ks, kr, mss, msr, zs, zr, bs, br, rs, rr, fs, fr,
):
    tok = lax.axis_index("tok")
    core, chip = tok % 2, tok // 2
    side, plane = chip % 2, chip // 2
    planes = count // 4
    other = 1 - core
    mate = tok + 1 - 2 * core
    across = 2 * (chip + 1 - 2 * side)
    step = 4 * (1 - 2 * side)
    fwd, src = tok + step, tok - step
    has_low, has_high = plane > 0, plane < planes - 1
    has_fwd = jnp.logical_or(jnp.logical_and(side == 0, has_high), jnp.logical_and(side == 1, has_low))
    has_src = jnp.logical_or(jnp.logical_and(side == 0, has_low), jnp.logical_and(side == 1, has_high))
    width = q_in.shape[1]
    dim = width // HEADS
    half_width = width // 2
    scale = dim ** -0.5

    barrier = pltpu.get_barrier_semaphore()

    def greet(target):
        pl.semaphore_signal(barrier, inc=1, device_id={"tok": target}, device_id_type=MESH)

    greet(mate)
    greet(across)
    greet(across + 1)

    @pl.when(has_fwd)
    def _():
        greet(fwd)
        greet(fwd + other - core)

    @pl.when(has_src)
    def _():
        greet(src)
        greet(src + other - core)

    def load(i, src_ref, dst_ref):
        return pltpu.make_async_copy(src_ref, dst_ref, ins.at[i])

    loads = [load(0, q_hbm, q_in), load(1, g_hbm, g_in), load(2, o_hbm, o_in), load(3, k_hbm, k_in), load(4, v_hbm, v_in),
             load(5, lse_hbm, lse_ref), load(6, keep_hbm, keep_ref)]
    for copy in loads:
        copy.start()

    def remote(src_ref, dst_ref, send, recv, target):
        return pltpu.make_async_remote_copy(
            src_ref=src_ref, dst_ref=dst_ref, send_sem=send, recv_sem=recv,
            device_id={"tok": target}, device_id_type=MESH,
        )

    def x_near(j):
        return remote(qbuf.at[core, j], qbuf.at[2 + core, j], xs.at[0, j], xr.at[0, j], across + core)

    def x_cross(j):
        return remote(qaway.at[j], qbuf.at[2 + core, j], xs.at[1, j], xr.at[1, j], across + other)

    def x_stat(i):
        return remote(sbuf.at[core] if i == 0 else saway, sbuf.at[2 + core], xss.at[i], xsr.at[i],
                      across + (core if i == 0 else other))

    def x_in(i, j):
        parity = core if i == 0 else other
        return remote(qaway.at[0], qbuf.at[2 + parity, j], xs.at[i, j], xr.at[i, j], across)

    def x_stat_in(i):
        parity = core if i == 0 else other
        return remote(saway, sbuf.at[2 + parity], xss.at[i], xsr.at[i], across)

    def m_q(j):
        return remote(qaway.at[j], qbuf.at[core, j], ms.at[j], mr.at[j], mate)

    def m_k(j):
        return remote(kaway.at[j], kbuf.at[core, j], ks.at[j], kr.at[j], mate)

    def m_stat():
        return remote(saway, sbuf.at[core], mss, msr, mate)

    def m_q_in(j):
        return remote(qaway.at[0], qbuf.at[other, j], ms.at[j], mr.at[j], mate)

    def m_k_in(j):
        return remote(kaway.at[0], kbuf.at[other, j], ks.at[j], kr.at[j], mate)

    def m_stat_in():
        return remote(saway, sbuf.at[other], mss, msr, mate)

    def z_k(i, j):
        return remote(kbuf.at[core, j] if i == 0 else kaway.at[j], kbuf.at[2 + core, j],
                      zs.at[i, j], zr.at[i, j], src + (0 if i == 0 else other - core))

    def z_k_in(i, j):
        parity = core if i == 0 else other
        return remote(kaway.at[0], kbuf.at[2 + parity, j], zs.at[i, j], zr.at[i, j], fwd)

    def z_back(j):
        return remote(zout.at[j], zback.at[j], bs.at[j], br.at[j], fwd)

    def z_back_in(j):
        return remote(zout.at[j], zback.at[j], bs.at[j], br.at[j], src)

    def rows(j):
        return pl.ds(pl.multiple_of(j * dim, 16), dim)

    def x_back(i, j):
        return remote(xout.at[i, j], xback.at[core, rows(j)], rs.at[i, j], rr.at[core, j], across + i)

    def x_back_in(i, j):
        return remote(xout.at[0, 0], xback.at[i, rows(j)], rs.at[i, j], rr.at[i, j], across)

    def m_back(j):
        return remote(mine.at[:, rows(j)], theirs.at[:, rows(j)], fs.at[j], fr.at[j], mate)

    def lanes(half, k):
        return pl.ds(pl.multiple_of(half * half_width + k * LANES, LANES), LANES)

    def pieces(k):
        at = k * LANES
        while at < (k + 1) * LANES:
            j = at // dim
            end = min((j + 1) * dim, (k + 1) * LANES)
            yield j, at - j * dim, end - j * dim, at - k * LANES, end - k * LANES
            at = end

    def flip(ref, k, near, far, i):
        for half, put in ((core, near), (other, far)):
            block = ref[:, lanes(half, k)].T
            for j, lo, hi, a, b in pieces(k):
                put(j, i, lo, hi, block[a:b])

    def q_near(j, i, lo, hi, x):
        qbuf[core, j, i, lo:hi] = x

    def q_far(j, i, lo, hi, x):
        qaway[j, i, lo:hi] = x

    def k_near(j, i, lo, hi, x):
        kbuf[core, j, i, lo:hi] = x

    def k_far(j, i, lo, hi, x):
        kaway[j, i, lo:hi] = x

    chunks = half_width // LANES
    ready = 0
    for k in range(chunks):
        if k == 0:
            loads[0].wait()
        flip(q_in, k, q_near, q_far, 0)
        if k == 0:
            loads[1].wait()
        flip(g_in, k, q_near, q_far, 1)
        if k == 0:
            pl.semaphore_wait(barrier, 3 + 2 * has_fwd.astype(jnp.int32) + 2 * has_src.astype(jnp.int32))
        done = (k + 1) * LANES // dim
        for j in range(ready, done):
            x_near(j).start()
            x_cross(j).start()
        for j in range(ready, done):
            m_q(j).start()
        ready = done
        if k == 0:
            loads[2].wait()
            loads[5].wait()
            head = lax.broadcasted_iota(jnp.int32, (HEADS, width), 0) * dim
            lane = lax.broadcasted_iota(jnp.int32, (HEADS, width), 1)
            pick = jnp.where(jnp.logical_and(lane >= head, lane < head + dim), 1.0, 0.0).astype(BF16)
            prod = g_in[...].astype(F32) * o_in[...].astype(F32)
            high = prod.astype(BF16)
            low = (prod - high.astype(F32)).astype(BF16)
            delta = dot_nt(pick, high) + dot_nt(pick, low)
            lse2 = lse_ref[...] * LOG2E
            first = core == 0
            sbuf[core, 0] = jnp.where(first, lse2[:HALF], lse2[HALF:])
            sbuf[core, 1] = jnp.where(first, delta[:HALF], delta[HALF:])
            saway[0] = jnp.where(first, lse2[HALF:], lse2[:HALF])
            saway[1] = jnp.where(first, delta[HALF:], delta[:HALF])
            x_stat(0).start()
            x_stat(1).start()
            m_stat().start()

    loads[3].wait()
    loads[4].wait()
    loads[6].wait()
    ready = 0
    for k in range(chunks):
        flip(k_in, k, k_near, k_far, 0)
        flip(v_in, k, k_near, k_far, 1)
        done = (k + 1) * LANES // dim
        for j in range(ready, done):
            m_k(j).start()

        @pl.when(has_src)
        def _():
            for j in range(ready, done):
                z_k(0, j).start()
                z_k(1, j).start()

        ready = done

    @pl.when(jnp.logical_not(has_src))
    def _():
        zback[...] = jnp.zeros(zback.shape, BF16)

    first_block = plane * 4 + side * 2
    across_block = plane * 4 + (1 - side) * 2

    def task(key, slot, query, j, keys, values):
        flag = keep_ref[key - query + 2, query]
        gone = (1 - flag).astype(F32) * 1e30
        q_t, g_t = qbuf[slot, j, 0], qbuf[slot, j, 1]
        lse = sbuf[slot, 0, pl.ds(j, 1), :] + gone
        delta = sbuf[slot, 1, pl.ds(j, 1), :]
        probs = jnp.exp2(dot_nn(keys, q_t) * (scale * LOG2E) - lse)
        grad = (probs * (dot_nn(values, g_t) - delta)).astype(BF16)
        return q_t, g_t, grad, probs.astype(BF16)

    def run(j, work):
        found, sums = {}, []
        for c, key, slots in work:
            keys_t = kbuf[c, j, 0]
            keys = keys_t.T
            values = kbuf[c, j, 1].T
            parts = [task(key, slot, query, j, keys, values) for slot, query, _ in slots]
            q_all, g_all, grads, lows = [jnp.concatenate([p[i] for p in parts], axis=1) for i in range(4)]
            sums.append((dot_nt(q_all, grads), dot_nt(g_all, lows)))
            for (_, _, name), p in zip(slots, parts):
                found.setdefault(name, []).append((keys_t, p[2]))
        out = {
            name: dot_nn(
                jnp.concatenate([t[0] for t in terms], axis=1),
                jnp.concatenate([t[1] for t in terms], axis=0),
            )
            for name, terms in found.items()
        }
        return out, sums

    def inner(j):
        m_q_in(j).wait_recv()
        m_k_in(j).wait_recv()

        @pl.when(j == 0)
        def _():
            m_stat_in().wait_recv()

        queries = [(b, first_block + b, b) for b in range(2)]
        got, sums = run(j, [(c, first_block + c, queries) for c in range(2)])
        for b in range(2):
            dqo[b, j] = got[b]
            dkv[j, b, 0] = sums[b][0]
            dkv[j, b, 1] = sums[b][1]

    near = (2 + side, across_block + side, 0)
    far = (3 - side, across_block + 1 - side, 1)
    close = 1 - side
    local = [(close, first_block + close, [near, far]), (1 - close, first_block + 1 - close, [near])]
    beyond = [(2 + side, first_block + step + side, [near, far]), (3 - side, first_block + step + 1 - side, [far])]

    def x_run(j):
        x_in(0, j).wait_recv()
        x_in(1, j).wait_recv()

        @pl.when(j == 0)
        def _():
            x_stat_in(0).wait_recv()
            x_stat_in(1).wait_recv()

        def finish(got, sums):
            for i, c in enumerate((close, 1 - close)):
                dkv[j, c, 0] += sums[i][0]
                dkv[j, c, 1] += sums[i][1]
            xout[side, j] = (got[0] * scale).astype(BF16)
            xout[1 - side, j] = (got[1] * scale).astype(BF16)

        @pl.when(has_fwd)
        def _():
            z_k_in(0, j).wait_recv()
            z_k_in(1, j).wait_recv()
            got, sums = run(j, local + beyond)
            finish(got, sums[:2])
            for i, c in enumerate((side, 1 - side)):
                zout[j, c, 0] = (sums[2 + i][0] * scale).astype(BF16)
                zout[j, c, 1] = sums[2 + i][1].astype(BF16)
            z_back(j).start()

        @pl.when(jnp.logical_not(has_fwd))
        def _():
            finish(*run(j, local))

        x_back(0, j).start()
        x_back(1, j).start()

    def share(j):
        @pl.when(has_src)
        def _():
            z_back_in(j).wait_recv()

        def total(c):
            return ((dkv[j, c, 0] * scale + zback[j, c, 0].astype(F32)).astype(BF16),
                    (dkv[j, c, 1] + zback[j, c, 1].astype(F32)).astype(BF16))

        mine[0, rows(j)] = (dqo[other, j] * scale).astype(BF16)
        mine[1, rows(j)], mine[2, rows(j)] = total(other)
        m_back(j).start()
        own[0, rows(j)], own[1, rows(j)] = total(core)

    for j in range(AHEAD):
        inner(j)

    @pl.loop(0, HALF)
    def _(i):
        x_run(i)

        @pl.when(i + AHEAD < HALF)
        def _():
            inner(i + AHEAD)

        @pl.when(i >= LAG)
        def _():
            share(i - LAG)

    for j in range(HALF - LAG, HALF):
        share(j)

    def put(out, half, k, x):
        out[:, lanes(half, k)] = x.T

    for j in range(HALF):
        m_back(j).wait_recv()
    for k in range(chunks):
        part = pl.ds(k * LANES, LANES)
        put(dk_out, core, k, own[0, part])
        put(dk_out, other, k, theirs[1, part])
        put(dv_out, core, k, own[1, part])
        put(dv_out, other, k, theirs[2, part])

    ready = 0
    for k in range(chunks):
        done = -(-(k + 1) * LANES // dim)
        for j in range(ready, done):
            x_back_in(0, j).wait_recv()
            x_back_in(1, j).wait_recv()
            own[0, rows(j)] = (dqo[core, j] * scale + xback[core, rows(j)].astype(F32)).astype(BF16)
        ready = done
        part = pl.ds(k * LANES, LANES)
        put(dq_out, core, k, own[0, part])
        put(dq_out, other, k, (theirs[0, part].astype(F32) + xback[other, part].astype(F32)).astype(BF16))

    for i in range(2):
        x_stat(i).wait_send()
    m_stat().wait_send()

    @pl.loop(0, HALF)
    def _(j):
        x_near(j).wait_send()
        x_cross(j).wait_send()
        m_q(j).wait_send()
        m_k(j).wait_send()
        m_back(j).wait_send()
        x_back(0, j).wait_send()
        x_back(1, j).wait_send()

        @pl.when(has_src)
        def _():
            z_k(0, j).wait_send()
            z_k(1, j).wait_send()

        @pl.when(has_fwd)
        def _():
            z_back(j).wait_send()


def store(a, b, c, x, y, z, sems):
    copies = [pltpu.make_async_copy(s, d, sems.at[i]) for i, (s, d) in enumerate(((a, x), (b, y), (c, z)))]
    for copy in copies:
        copy.start()
    for copy in copies:
        copy.wait()


def per_device(count, query_rows, key_rows, value_rows, out_rows, grad_out, normalizer, keep_tasks):
    block, width = query_rows.shape
    dim = width // HEADS
    half = width // 2
    vmem = pl.BlockSpec(memory_space=pltpu.VMEM)
    hbm = pl.BlockSpec(memory_space=pl.ANY)
    dma = pltpu.SemaphoreType.DMA
    outs = [jax.ShapeDtypeStruct((block, width), BF16)] * 3
    packed = pl.pallas_call(
        functools.partial(kernel, count),
        out_shape=[pltpu.VMEM((block, width), BF16)] * 3,
        in_specs=[hbm] * 7,
        out_specs=[vmem] * 3,
        scratch_shapes=[
            *[pltpu.VMEM((block, width), BF16)] * 5,
            pltpu.VMEM(normalizer.shape, F32),
            pltpu.SMEM(keep_tasks.shape[::-1], jnp.int32),
            pltpu.VMEM((4, HALF, 2, dim, block), BF16),
            pltpu.VMEM((HALF, 2, dim, block), BF16),
            pltpu.VMEM((4, HALF, 2, dim, block), BF16),
            pltpu.VMEM((HALF, 2, dim, block), BF16),
            pltpu.VMEM((4, 2, HALF, block), F32),
            pltpu.VMEM((2, HALF, block), F32),
            pltpu.VMEM((2, HALF, dim, block), F32),
            pltpu.VMEM((HALF, 2, 2, dim, block), F32),
            pltpu.VMEM((HALF, 2, 2, dim, block), BF16),
            pltpu.VMEM((HALF, 2, 2, dim, block), BF16),
            pltpu.VMEM((2, HALF, dim, block), BF16),
            pltpu.VMEM((2, half, block), BF16),
            pltpu.VMEM((2, half, block), BF16),
            pltpu.VMEM((3, half, block), BF16),
            pltpu.VMEM((3, half, block), BF16),
            dma((7,)),
            dma((2, HALF)), dma((2, HALF)), dma((2,)), dma((2,)),
            dma((HALF,)), dma((HALF,)), dma((HALF,)), dma((HALF,)), dma, dma,
            dma((2, HALF)), dma((2, HALF)),
            dma((HALF,)), dma((HALF,)),
            dma((2, HALF)), dma((2, HALF)),
            dma((HALF,)), dma((HALF,)),
        ],
        compiler_params=pltpu.CompilerParams(
            collective_id=0, has_side_effects=True, vmem_limit_bytes=40 * 1024 * 1024
        ),
    )(*[pltpu.with_memory_space_constraint(x, pltpu.HBM) for x in (query_rows, key_rows, value_rows, out_rows, grad_out, normalizer, keep_tasks.T)])
    return pl.pallas_call(
        store,
        out_shape=outs,
        in_specs=[vmem] * 3,
        out_specs=[hbm] * 3,
        scratch_shapes=[dma((3,))],
    )(*[pltpu.with_memory_space_constraint(x, pltpu.VMEM) for x in packed])


def solution(mesh):
    rows = P(("groups", "tok"), None)
    return jax.shard_map(
        functools.partial(per_device, mesh.shape["tok"]),
        mesh=mesh,
        in_specs=(rows,) * 5 + (P(None, ("groups", "tok")), P("groups", None)),
        out_specs=(rows,) * 3,
        check_vma=False,
    )
```

```python
import functools

import jax
import jax.numpy as jnp
from jax import lax
from jax.experimental import pallas as pl
from jax.experimental.pallas import tpu as pltpu
from jax.sharding import PartitionSpec as P

HEADS = 16
HALF = HEADS // 2
LANES = 128
LOG2E = 1.4426950408889634
MESH = pl.DeviceIdType.MESH
F32 = jnp.float32
BF16 = jnp.bfloat16
AHEAD = 4
LAG = 3
PAIR = 2


def dot_nn(a, b):
    return lax.dot_general(a, b, (((1,), (0,)), ((), ())), preferred_element_type=F32)


def dot_nt(a, b):
    return lax.dot_general(a, b, (((1,), (1,)), ((), ())), preferred_element_type=F32)


def kernel(
    count, q_hbm, k_hbm, v_hbm, o_hbm, g_hbm, lse_hbm, keep_hbm,
    dq_out, dk_out, dv_out,
    q_in, k_in, v_in, o_in, g_in, lse_ref, keep_ref,
    qbuf, qaway, kbuf, kaway, sbuf, saway, dqo, dkv,
    zout, zback, xout, xback, own, mine, theirs,
    ins, xs, xr, xss, xsr, ms, mr, ks, kr, mss, msr, zs, zr, bs, br, rs, rr, fs, fr,
):
    tok = lax.axis_index("tok")
    core, chip = tok % 2, tok // 2
    side, plane = chip % 2, chip // 2
    planes = count // 4
    other = 1 - core
    mate = tok + 1 - 2 * core
    across = 2 * (chip + 1 - 2 * side)
    step = 4 * (1 - 2 * side)
    fwd, src = tok + step, tok - step
    has_low, has_high = plane > 0, plane < planes - 1
    has_fwd = jnp.logical_or(jnp.logical_and(side == 0, has_high), jnp.logical_and(side == 1, has_low))
    has_src = jnp.logical_or(jnp.logical_and(side == 0, has_low), jnp.logical_and(side == 1, has_high))
    width = q_in.shape[1]
    dim = width // HEADS
    scale = dim ** -0.5

    barrier = pltpu.get_barrier_semaphore()

    def greet(target):
        pl.semaphore_signal(barrier, inc=1, device_id={"tok": target}, device_id_type=MESH)

    greet(mate)
    greet(across)
    greet(across + 1)

    @pl.when(has_fwd)
    def _():
        greet(fwd)
        greet(fwd + other - core)

    @pl.when(has_src)
    def _():
        greet(src)
        greet(src + other - core)

    half_width = q_in.shape[1] // 2
    loads = []

    def load(src_ref, dst_ref):
        copy = pltpu.make_async_copy(src_ref, dst_ref, ins.at[len(loads)])
        copy.start()
        loads.append(copy)

    for lo, hi in ((0, LANES), (LANES, half_width)):
        for src_ref, dst_ref in ((q_hbm, q_in), (g_hbm, g_in)):
            for base in (0, half_width):
                part = (slice(None), pl.ds(base + lo, hi - lo))
                load(src_ref.at[part], dst_ref.at[part])
    for src_ref, dst_ref in ((o_hbm, o_in), (lse_hbm, lse_ref), (k_hbm, k_in), (v_hbm, v_in), (keep_hbm, keep_ref)):
        load(src_ref, dst_ref)

    def remote(src_ref, dst_ref, send, recv, target):
        return pltpu.make_async_remote_copy(
            src_ref=src_ref, dst_ref=dst_ref, send_sem=send, recv_sem=recv,
            device_id={"tok": target}, device_id_type=MESH,
        )

    def x_near(j):
        return remote(qbuf.at[core, j], qbuf.at[2 + core, j], xs.at[0, j], xr.at[0, j], across + core)

    def x_cross(j):
        return remote(qaway.at[j], qbuf.at[2 + core, j], xs.at[1, j], xr.at[1, j], across + other)

    def x_stat(i):
        return remote(sbuf.at[core] if i == 0 else saway, sbuf.at[2 + core], xss.at[i], xsr.at[i],
                      across + (core if i == 0 else other))

    def x_in(i, j):
        parity = core if i == 0 else other
        return remote(qaway.at[0], qbuf.at[2 + parity, j], xs.at[i, j], xr.at[i, j], across)

    def x_stat_in(i):
        parity = core if i == 0 else other
        return remote(saway, sbuf.at[2 + parity], xss.at[i], xsr.at[i], across)

    def m_q(j):
        return remote(qaway.at[j], qbuf.at[core, j], ms.at[j], mr.at[j], mate)

    def m_k(j):
        return remote(kaway.at[j], kbuf.at[core, j], ks.at[j], kr.at[j], mate)

    def m_stat():
        return remote(saway, sbuf.at[core], mss, msr, mate)

    def m_q_in(j):
        return remote(qaway.at[0], qbuf.at[other, j], ms.at[j], mr.at[j], mate)

    def m_k_in(j):
        return remote(kaway.at[0], kbuf.at[other, j], ks.at[j], kr.at[j], mate)

    def m_stat_in():
        return remote(saway, sbuf.at[other], mss, msr, mate)

    def z_k(i, j):
        return remote(kbuf.at[core, j] if i == 0 else kaway.at[j], kbuf.at[2 + core, j],
                      zs.at[i, j], zr.at[i, j], src + (0 if i == 0 else other - core))

    def z_k_in(i, j):
        parity = core if i == 0 else other
        return remote(kaway.at[0], kbuf.at[2 + parity, j], zs.at[i, j], zr.at[i, j], fwd)

    def z_back(j):
        return remote(zout.at[j], zback.at[j], bs.at[j], br.at[j], fwd)

    def z_back_in(j):
        return remote(zout.at[j], zback.at[j], bs.at[j], br.at[j], src)

    def rows(j, n=1):
        return pl.ds(pl.multiple_of(j * dim, 16), n * dim)

    def x_back(i, j):
        part = rows(j * PAIR, PAIR)
        return remote(xout.at[i, part], xback.at[core, part], rs.at[i, j], rr.at[core, j], across + i)

    def x_back_in(i, j):
        part = rows(j * PAIR, PAIR)
        return remote(xout.at[0, part], xback.at[i, part], rs.at[i, j], rr.at[i, j], across)

    def m_back(j):
        return remote(mine.at[:, rows(j)], theirs.at[:, rows(j)], fs.at[j], fr.at[j], mate)

    def lanes(half, k):
        return pl.ds(pl.multiple_of(half * half_width + k * LANES, LANES), LANES)

    def pieces(k):
        at = k * LANES
        while at < (k + 1) * LANES:
            j = at // dim
            end = min((j + 1) * dim, (k + 1) * LANES)
            yield j, at - j * dim, end - j * dim, at - k * LANES, end - k * LANES
            at = end

    def flip(ref, k, near, far, i):
        for half, put in ((core, near), (other, far)):
            block = ref[:, lanes(half, k)].T
            for j, lo, hi, a, b in pieces(k):
                put(j, i, lo, hi, block[a:b])

    def q_near(j, i, lo, hi, x):
        qbuf[core, j, i, lo:hi] = x

    def q_far(j, i, lo, hi, x):
        qaway[j, i, lo:hi] = x

    def k_near(j, i, lo, hi, x):
        kbuf[core, j, i, lo:hi] = x

    def k_far(j, i, lo, hi, x):
        kaway[j, i, lo:hi] = x

    chunks = half_width // LANES
    ready = 0
    for k in range(chunks):
        if k == 0:
            for copy in loads[:4]:
                copy.wait()
        flip(q_in, k, q_near, q_far, 0)
        flip(g_in, k, q_near, q_far, 1)
        if k == 0:
            pl.semaphore_wait(barrier, 3 + 2 * has_fwd.astype(jnp.int32) + 2 * has_src.astype(jnp.int32))
        done = (k + 1) * LANES // dim
        for j in range(ready, done):
            x_near(j).start()
            x_cross(j).start()
        for j in range(ready, done):
            m_q(j).start()
        ready = done
        if k == 0:
            for copy in loads[4:10]:
                copy.wait()
            head = lax.broadcasted_iota(jnp.int32, (HEADS, width), 0) * dim
            lane = lax.broadcasted_iota(jnp.int32, (HEADS, width), 1)
            pick = jnp.where(jnp.logical_and(lane >= head, lane < head + dim), 1.0, 0.0).astype(BF16)
            prod = g_in[...].astype(F32) * o_in[...].astype(F32)
            high = prod.astype(BF16)
            low = (prod - high.astype(F32)).astype(BF16)
            delta = dot_nt(pick, high) + dot_nt(pick, low)
            lse2 = lse_ref[...] * LOG2E
            first = core == 0
            sbuf[core, 0] = jnp.where(first, lse2[:HALF], lse2[HALF:])
            sbuf[core, 1] = jnp.where(first, delta[:HALF], delta[HALF:])
            saway[0] = jnp.where(first, lse2[HALF:], lse2[:HALF])
            saway[1] = jnp.where(first, delta[HALF:], delta[:HALF])
            x_stat(0).start()
            x_stat(1).start()
            m_stat().start()

    for copy in loads[10:]:
        copy.wait()
    ready = 0
    for k in range(chunks):
        flip(k_in, k, k_near, k_far, 0)
        flip(v_in, k, k_near, k_far, 1)
        done = (k + 1) * LANES // dim
        for j in range(ready, done):
            m_k(j).start()

        @pl.when(has_src)
        def _():
            for j in range(ready, done):
                z_k(0, j).start()
                z_k(1, j).start()

        ready = done

    @pl.when(jnp.logical_not(has_src))
    def _():
        zback[...] = jnp.zeros(zback.shape, BF16)

    first_block = plane * 4 + side * 2
    across_block = plane * 4 + (1 - side) * 2

    def task(key, slot, query, j, keys, values):
        flag = keep_ref[key - query + 2, query]
        gone = (1 - flag).astype(F32) * 1e30
        q_t, g_t = qbuf[slot, j, 0], qbuf[slot, j, 1]
        lse = sbuf[slot, 0, pl.ds(j, 1), :] + gone
        delta = sbuf[slot, 1, pl.ds(j, 1), :]
        probs = jnp.exp2(dot_nn(keys, q_t) * (scale * LOG2E) - lse)
        grad = (probs * (dot_nn(values, g_t) - delta)).astype(BF16)
        return q_t, g_t, grad, probs.astype(BF16)

    def run(j, work):
        found, sums = {}, []
        for c, key, slots in work:
            keys_t = kbuf[c, j, 0]
            keys = keys_t.T
            values = kbuf[c, j, 1].T
            parts = [task(key, slot, query, j, keys, values) for slot, query, _ in slots]
            q_all, g_all, grads, lows = [jnp.concatenate([p[i] for p in parts], axis=1) for i in range(4)]
            sums.append((dot_nt(q_all, grads), dot_nt(g_all, lows)))
            for (_, _, name), p in zip(slots, parts):
                found.setdefault(name, []).append((keys_t, p[2]))
        out = {
            name: dot_nn(
                jnp.concatenate([t[0] for t in terms], axis=1),
                jnp.concatenate([t[1] for t in terms], axis=0),
            )
            for name, terms in found.items()
        }
        return out, sums

    def inner(j):
        m_q_in(j).wait_recv()
        m_k_in(j).wait_recv()

        @pl.when(j == 0)
        def _():
            m_stat_in().wait_recv()

        queries = [(b, first_block + b, b) for b in range(2)]
        got, sums = run(j, [(c, first_block + c, queries) for c in range(2)])
        for b in range(2):
            dqo[b, rows(j)] = got[b]
            dkv[j, b, 0] = sums[b][0]
            dkv[j, b, 1] = sums[b][1]

    near = (2 + side, across_block + side, 0)
    far = (3 - side, across_block + 1 - side, 1)
    close = 1 - side
    local = [(close, first_block + close, [near, far]), (1 - close, first_block + 1 - close, [near])]
    beyond = [(2 + side, first_block + step + side, [near, far]), (3 - side, first_block + step + 1 - side, [far])]

    def x_run(j):
        x_in(0, j).wait_recv()
        x_in(1, j).wait_recv()

        @pl.when(j == 0)
        def _():
            x_stat_in(0).wait_recv()
            x_stat_in(1).wait_recv()

        def finish(got, sums):
            for i, c in enumerate((close, 1 - close)):
                dkv[j, c, 0] += sums[i][0]
                dkv[j, c, 1] += sums[i][1]
            xout[side, rows(j)] = (got[0] * scale).astype(BF16)
            xout[1 - side, rows(j)] = (got[1] * scale).astype(BF16)

        @pl.when(has_fwd)
        def _():
            z_k_in(0, j).wait_recv()
            z_k_in(1, j).wait_recv()
            got, sums = run(j, local + beyond)
            finish(got, sums[:2])
            for i, c in enumerate((side, 1 - side)):
                zout[j, c, 0] = (sums[2 + i][0] * scale).astype(BF16)
                zout[j, c, 1] = sums[2 + i][1].astype(BF16)
            z_back(j).start()

        @pl.when(jnp.logical_not(has_fwd))
        def _():
            finish(*run(j, local))

        @pl.when(j % PAIR == PAIR - 1)
        def _():
            x_back(0, j // PAIR).start()
            x_back(1, j // PAIR).start()

    def share(j):
        @pl.when(has_src)
        def _():
            z_back_in(j).wait_recv()

        def total(c):
            return ((dkv[j, c, 0] * scale + zback[j, c, 0].astype(F32)).astype(BF16),
                    (dkv[j, c, 1] + zback[j, c, 1].astype(F32)).astype(BF16))

        mine[0, rows(j)] = (dqo[other, rows(j)] * scale).astype(BF16)
        mine[1, rows(j)], mine[2, rows(j)] = total(other)
        m_back(j).start()
        own[0, rows(j)], own[1, rows(j)] = total(core)

    for j in range(AHEAD):
        inner(j)

    @pl.loop(0, HALF)
    def _(i):
        x_run(i)

        @pl.when(i + AHEAD < HALF)
        def _():
            inner(i + AHEAD)

        @pl.when(i >= LAG)
        def _():
            share(i - LAG)

    for j in range(HALF - LAG, HALF):
        share(j)

    def put(out, half, k, x):
        out[:, lanes(half, k)] = x.T

    for j in range(HALF):
        m_back(j).wait_recv()
    for k in range(chunks):
        part = pl.ds(k * LANES, LANES)
        put(dk_out, core, k, own[0, part])
        put(dk_out, other, k, theirs[1, part])
        put(dv_out, core, k, own[1, part])
        put(dv_out, other, k, theirs[2, part])

    for i in range(2):
        x_stat(i).wait_send()
    m_stat().wait_send()

    @pl.loop(0, HALF)
    def _(j):
        x_near(j).wait_send()
        x_cross(j).wait_send()
        m_q(j).wait_send()
        m_k(j).wait_send()
        m_back(j).wait_send()

        @pl.when(has_src)
        def _():
            z_k(0, j).wait_send()
            z_k(1, j).wait_send()

        @pl.when(has_fwd)
        def _():
            z_back(j).wait_send()

    ready = 0
    for k in range(chunks):
        done = -(-(k + 1) * LANES // (dim * PAIR))
        for j in range(ready, done):
            part = rows(j * PAIR, PAIR)
            for i in range(2):
                x_back(i, j).wait_send()
                x_back_in(i, j).wait_recv()
        ready = done
        part = pl.ds(k * LANES, LANES)
        put(dq_out, core, k, (dqo[core, part] * scale + xback[core, part].astype(F32)).astype(BF16))
        put(dq_out, other, k, (theirs[0, part].astype(F32) + xback[other, part].astype(F32)).astype(BF16))


def store(a, b, c, x, y, z, sems):
    copies = [pltpu.make_async_copy(s, d, sems.at[i]) for i, (s, d) in enumerate(((a, x), (b, y), (c, z)))]
    for copy in copies:
        copy.start()
    for copy in copies:
        copy.wait()


def per_device(count, query_rows, key_rows, value_rows, out_rows, grad_out, normalizer, keep_tasks):
    block, width = query_rows.shape
    dim = width // HEADS
    half = width // 2
    vmem = pl.BlockSpec(memory_space=pltpu.VMEM)
    hbm = pl.BlockSpec(memory_space=pl.ANY)
    dma = pltpu.SemaphoreType.DMA
    outs = [jax.ShapeDtypeStruct((block, width), BF16)] * 3
    packed = pl.pallas_call(
        functools.partial(kernel, count),
        out_shape=[pltpu.VMEM((block, width), BF16)] * 3,
        in_specs=[hbm] * 7,
        out_specs=[vmem] * 3,
        scratch_shapes=[
            *[pltpu.VMEM((block, width), BF16)] * 5,
            pltpu.VMEM(normalizer.shape, F32),
            pltpu.SMEM(keep_tasks.shape[::-1], jnp.int32),
            pltpu.VMEM((4, HALF, 2, dim, block), BF16),
            pltpu.VMEM((HALF, 2, dim, block), BF16),
            pltpu.VMEM((4, HALF, 2, dim, block), BF16),
            pltpu.VMEM((HALF, 2, dim, block), BF16),
            pltpu.VMEM((4, 2, HALF, block), F32),
            pltpu.VMEM((2, HALF, block), F32),
            pltpu.VMEM((2, half, block), F32),
            pltpu.VMEM((HALF, 2, 2, dim, block), F32),
            pltpu.VMEM((HALF, 2, 2, dim, block), BF16),
            pltpu.VMEM((HALF, 2, 2, dim, block), BF16),
            *[pltpu.VMEM((2, half, block), BF16)] * 3,
            pltpu.VMEM((3, half, block), BF16),
            pltpu.VMEM((3, half, block), BF16),
            dma((13,)),
            dma((2, HALF)), dma((2, HALF)), dma((2,)), dma((2,)),
            dma((HALF,)), dma((HALF,)), dma((HALF,)), dma((HALF,)), dma, dma,
            dma((2, HALF)), dma((2, HALF)),
            dma((HALF,)), dma((HALF,)),
            dma((2, HALF // PAIR)), dma((2, HALF // PAIR)),
            dma((HALF,)), dma((HALF,)),
        ],
        compiler_params=pltpu.CompilerParams(
            collective_id=0, has_side_effects=True, vmem_limit_bytes=40 * 1024 * 1024
        ),
    )(*[pltpu.with_memory_space_constraint(x, pltpu.HBM) for x in (query_rows, key_rows, value_rows, out_rows, grad_out, normalizer, keep_tasks.T)])
    return pl.pallas_call(
        store,
        out_shape=outs,
        in_specs=[vmem] * 3,
        out_specs=[hbm] * 3,
        scratch_shapes=[dma((3,))],
    )(*[pltpu.with_memory_space_constraint(x, pltpu.VMEM) for x in packed])


def solution(mesh):
    rows = P(("groups", "tok"), None)
    return jax.shard_map(
        functools.partial(per_device, mesh.shape["tok"]),
        mesh=mesh,
        in_specs=(rows,) * 5 + (P(None, ("groups", "tok")), P("groups", None)),
        out_specs=(rows,) * 3,
        check_vma=False,
    )
```

```python
import functools

import jax
import jax.numpy as jnp
from jax import lax
from jax.experimental import pallas as pl
from jax.experimental.pallas import tpu as pltpu
from jax.sharding import PartitionSpec as P

HEADS = 16
HALF = HEADS // 2
LANES = 128
LOG2E = 1.4426950408889634
MESH = pl.DeviceIdType.MESH
F32 = jnp.float32
BF16 = jnp.bfloat16
AHEAD = 4
LAG = 3
PAIR = 2


def dot_nn(a, b):
    return lax.dot_general(a, b, (((1,), (0,)), ((), ())), preferred_element_type=F32)


def dot_nt(a, b):
    return lax.dot_general(a, b, (((1,), (1,)), ((), ())), preferred_element_type=F32)


def kernel(
    count, q_hbm, k_hbm, v_hbm, o_hbm, g_hbm, lse_hbm, keep_hbm,
    dq_out, dk_out, dv_out,
    q_in, k_in, v_in, o_in, g_in, lse_ref, keep_ref,
    qbuf, qaway, kbuf, kaway, sbuf, saway, dqo, dkv,
    zout, zback, xout, xback, own, mine, theirs,
    ins, xs, xr, xss, xsr, ms, mr, ks, kr, mss, msr, zs, zr, bs, br, rs, rr, fs, fr,
):
    tok = lax.axis_index("tok")
    core, chip = tok % 2, tok // 2
    side, plane = chip % 2, chip // 2
    planes = count // 4
    other = 1 - core
    mate = tok + 1 - 2 * core
    across = 2 * (chip + 1 - 2 * side)
    step = 4 * (1 - 2 * side)
    fwd, src = tok + step, tok - step
    has_low, has_high = plane > 0, plane < planes - 1
    has_fwd = jnp.logical_or(jnp.logical_and(side == 0, has_high), jnp.logical_and(side == 1, has_low))
    has_src = jnp.logical_or(jnp.logical_and(side == 0, has_low), jnp.logical_and(side == 1, has_high))
    width = q_in.shape[1]
    dim = width // HEADS
    scale = dim ** -0.5

    barrier = pltpu.get_barrier_semaphore()

    def greet(target):
        pl.semaphore_signal(barrier, inc=1, device_id={"tok": target}, device_id_type=MESH)

    greet(mate)
    greet(across)
    greet(across + 1)

    @pl.when(has_fwd)
    def _():
        greet(fwd)
        greet(fwd + other - core)

    @pl.when(has_src)
    def _():
        greet(src)
        greet(src + other - core)

    half_width = q_in.shape[1] // 2
    loads = []

    def load(src_ref, dst_ref):
        copy = pltpu.make_async_copy(src_ref, dst_ref, ins.at[len(loads)])
        copy.start()
        loads.append(copy)

    for lo, hi in ((0, LANES), (LANES, half_width)):
        for src_ref, dst_ref in ((q_hbm, q_in), (g_hbm, g_in)):
            for base in (0, half_width):
                part = (slice(None), pl.ds(base + lo, hi - lo))
                load(src_ref.at[part], dst_ref.at[part])
    for src_ref, dst_ref in ((o_hbm, o_in), (lse_hbm, lse_ref), (k_hbm, k_in), (v_hbm, v_in), (keep_hbm, keep_ref)):
        load(src_ref, dst_ref)

    def remote(src_ref, dst_ref, send, recv, target):
        return pltpu.make_async_remote_copy(
            src_ref=src_ref, dst_ref=dst_ref, send_sem=send, recv_sem=recv,
            device_id={"tok": target}, device_id_type=MESH,
        )

    def x_near(j):
        return remote(qbuf.at[core, j], qbuf.at[2 + core, j], xs.at[0, j], xr.at[0, j], across + core)

    def x_cross(j):
        return remote(qaway.at[j], qbuf.at[2 + core, j], xs.at[1, j], xr.at[1, j], across + other)

    def x_stat(i):
        return remote(sbuf.at[core] if i == 0 else saway, sbuf.at[2 + core], xss.at[i], xsr.at[i],
                      across + (core if i == 0 else other))

    def x_in(i, j):
        parity = core if i == 0 else other
        return remote(qaway.at[0], qbuf.at[2 + parity, j], xs.at[i, j], xr.at[i, j], across)

    def x_stat_in(i):
        parity = core if i == 0 else other
        return remote(saway, sbuf.at[2 + parity], xss.at[i], xsr.at[i], across)

    def m_q(j):
        return remote(qaway.at[j], qbuf.at[core, j], ms.at[j], mr.at[j], mate)

    def m_k(j):
        return remote(kaway.at[j], kbuf.at[core, j], ks.at[j], kr.at[j], mate)

    def m_stat():
        return remote(saway, sbuf.at[core], mss, msr, mate)

    def m_q_in(j):
        return remote(qaway.at[0], qbuf.at[other, j], ms.at[j], mr.at[j], mate)

    def m_k_in(j):
        return remote(kaway.at[0], kbuf.at[other, j], ks.at[j], kr.at[j], mate)

    def m_stat_in():
        return remote(saway, sbuf.at[other], mss, msr, mate)

    def z_k(i, j):
        return remote(kbuf.at[core, j] if i == 0 else kaway.at[j], kbuf.at[2 + core, j],
                      zs.at[i, j], zr.at[i, j], src + (0 if i == 0 else other - core))

    def z_k_in(i, j):
        parity = core if i == 0 else other
        return remote(kaway.at[0], kbuf.at[2 + parity, j], zs.at[i, j], zr.at[i, j], fwd)

    def z_back(j):
        return remote(zout.at[j], zback.at[j], bs.at[j], br.at[j], fwd)

    def z_back_in(j):
        return remote(zout.at[j], zback.at[j], bs.at[j], br.at[j], src)

    def rows(j, n=1):
        return pl.ds(pl.multiple_of(j * dim, 16), n * dim)

    def x_back(i, j):
        part = rows(j * PAIR, PAIR)
        return remote(xout.at[i, part], xback.at[core, part], rs.at[i, j], rr.at[core, j], across + i)

    def x_back_in(i, j):
        part = rows(j * PAIR, PAIR)
        return remote(xout.at[0, part], xback.at[i, part], rs.at[i, j], rr.at[i, j], across)

    def m_back(j):
        return remote(mine.at[:, rows(j)], theirs.at[:, rows(j)], fs.at[j], fr.at[j], mate)

    def lanes(half, k):
        return pl.ds(pl.multiple_of(half * half_width + k * LANES, LANES), LANES)

    def pieces(k):
        at = k * LANES
        while at < (k + 1) * LANES:
            j = at // dim
            end = min((j + 1) * dim, (k + 1) * LANES)
            yield j, at - j * dim, end - j * dim, at - k * LANES, end - k * LANES
            at = end

    def flip(ref, k, near, far, i):
        for half, put in ((core, near), (other, far)):
            block = ref[:, lanes(half, k)].T
            for j, lo, hi, a, b in pieces(k):
                put(j, i, lo, hi, block[a:b])

    def q_near(j, i, lo, hi, x):
        qbuf[core, j, i, lo:hi] = x

    def q_far(j, i, lo, hi, x):
        qaway[j, i, lo:hi] = x

    def k_near(j, i, lo, hi, x):
        kbuf[core, j, i, lo:hi] = x

    def k_far(j, i, lo, hi, x):
        kaway[j, i, lo:hi] = x

    chunks = half_width // LANES
    ready = 0
    for k in range(chunks):
        if k == 0:
            for copy in loads[:4]:
                copy.wait()
        flip(q_in, k, q_near, q_far, 0)
        flip(g_in, k, q_near, q_far, 1)
        if k == 0:
            pl.semaphore_wait(barrier, 3 + 2 * has_fwd.astype(jnp.int32) + 2 * has_src.astype(jnp.int32))
        done = (k + 1) * LANES // dim
        for j in range(ready, done):
            x_near(j).start()
            x_cross(j).start()
        for j in range(ready, done):
            m_q(j).start()
        ready = done
        if k == 0:
            for copy in loads[4:10]:
                copy.wait()
            head = lax.broadcasted_iota(jnp.int32, (HEADS, width), 0) * dim
            lane = lax.broadcasted_iota(jnp.int32, (HEADS, width), 1)
            pick = jnp.where(jnp.logical_and(lane >= head, lane < head + dim), 1.0, 0.0).astype(BF16)
            prod = g_in[...].astype(F32) * o_in[...].astype(F32)
            high = prod.astype(BF16)
            low = (prod - high.astype(F32)).astype(BF16)
            delta = dot_nt(pick, high) + dot_nt(pick, low)
            lse2 = lse_ref[...] * LOG2E
            first = core == 0
            sbuf[core, 0] = jnp.where(first, lse2[:HALF], lse2[HALF:])
            sbuf[core, 1] = jnp.where(first, delta[:HALF], delta[HALF:])
            saway[0] = jnp.where(first, lse2[HALF:], lse2[:HALF])
            saway[1] = jnp.where(first, delta[HALF:], delta[:HALF])
            x_stat(0).start()
            x_stat(1).start()
            m_stat().start()

    for copy in loads[10:]:
        copy.wait()
    ready = 0
    for k in range(chunks):
        flip(k_in, k, k_near, k_far, 0)
        flip(v_in, k, k_near, k_far, 1)
        done = (k + 1) * LANES // dim
        for j in range(ready, done):
            m_k(j).start()

        @pl.when(has_src)
        def _():
            for j in range(ready, done):
                z_k(0, j).start()
                z_k(1, j).start()

        ready = done

    @pl.when(jnp.logical_not(has_src))
    def _():
        zback[...] = jnp.zeros(zback.shape, BF16)

    first_block = plane * 4 + side * 2
    across_block = plane * 4 + (1 - side) * 2

    def task(key, slot, query, j, keys, values):
        flag = keep_ref[key - query + 2, query]
        gone = (1 - flag).astype(F32) * 1e30
        q_t, g_t = qbuf[slot, j, 0], qbuf[slot, j, 1]
        lse = sbuf[slot, 0, pl.ds(j, 1), :] + gone
        delta = sbuf[slot, 1, pl.ds(j, 1), :]
        probs = jnp.exp2(dot_nn(keys, q_t) * (scale * LOG2E) - lse)
        grad = (probs * (dot_nn(values, g_t) - delta)).astype(BF16)
        return q_t, g_t, grad, probs.astype(BF16)

    def run(j, work):
        found, sums = {}, []
        for c, key, slots in work:
            keys_t = kbuf[c, j, 0]
            keys = keys_t.T
            values = kbuf[c, j, 1].T
            parts = [task(key, slot, query, j, keys, values) for slot, query, _ in slots]
            q_all, g_all, grads, lows = [jnp.concatenate([p[i] for p in parts], axis=1) for i in range(4)]
            sums.append((dot_nn(grads, q_all.T).T, dot_nn(lows, g_all.T).T))
            for (_, _, name), p in zip(slots, parts):
                found.setdefault(name, []).append((keys_t, p[2]))
        out = {
            name: dot_nn(
                jnp.concatenate([t[0] for t in terms], axis=1),
                jnp.concatenate([t[1] for t in terms], axis=0),
            )
            for name, terms in found.items()
        }
        return out, sums

    def inner(j):
        m_q_in(j).wait_recv()
        m_k_in(j).wait_recv()

        @pl.when(j == 0)
        def _():
            m_stat_in().wait_recv()

        queries = [(b, first_block + b, b) for b in range(2)]
        got, sums = run(j, [(c, first_block + c, queries) for c in range(2)])
        for b in range(2):
            dqo[b, rows(j)] = got[b]
            dkv[j, b, 0] = sums[b][0]
            dkv[j, b, 1] = sums[b][1]

    near = (2 + side, across_block + side, 0)
    far = (3 - side, across_block + 1 - side, 1)
    close = 1 - side
    local = [(close, first_block + close, [near, far]), (1 - close, first_block + 1 - close, [near])]
    beyond = [(2 + side, first_block + step + side, [near, far]), (3 - side, first_block + step + 1 - side, [far])]

    def x_run(j):
        x_in(0, j).wait_recv()
        x_in(1, j).wait_recv()

        @pl.when(j == 0)
        def _():
            x_stat_in(0).wait_recv()
            x_stat_in(1).wait_recv()

        def finish(got, sums):
            for i, c in enumerate((close, 1 - close)):
                dkv[j, c, 0] += sums[i][0]
                dkv[j, c, 1] += sums[i][1]
            xout[side, rows(j)] = (got[0] * scale).astype(BF16)
            xout[1 - side, rows(j)] = (got[1] * scale).astype(BF16)

        @pl.when(has_fwd)
        def _():
            z_k_in(0, j).wait_recv()
            z_k_in(1, j).wait_recv()
            got, sums = run(j, local + beyond)
            finish(got, sums[:2])
            for i, c in enumerate((side, 1 - side)):
                zout[j, c, 0] = (sums[2 + i][0] * scale).astype(BF16)
                zout[j, c, 1] = sums[2 + i][1].astype(BF16)
            z_back(j).start()

        @pl.when(jnp.logical_not(has_fwd))
        def _():
            finish(*run(j, local))

        @pl.when(j % PAIR == PAIR - 1)
        def _():
            x_back(0, j // PAIR).start()
            x_back(1, j // PAIR).start()

    def share(j):
        @pl.when(has_src)
        def _():
            z_back_in(j).wait_recv()

        def total(c):
            return ((dkv[j, c, 0] * scale + zback[j, c, 0].astype(F32)).astype(BF16),
                    (dkv[j, c, 1] + zback[j, c, 1].astype(F32)).astype(BF16))

        mine[0, rows(j)] = (dqo[other, rows(j)] * scale).astype(BF16)
        mine[1, rows(j)], mine[2, rows(j)] = total(other)
        m_back(j).start()
        own[0, rows(j)], own[1, rows(j)] = total(core)

    for j in range(AHEAD):
        inner(j)

    @pl.loop(0, HALF)
    def _(i):
        x_run(i)

        @pl.when(i + AHEAD < HALF)
        def _():
            inner(i + AHEAD)

        @pl.when(i >= LAG)
        def _():
            share(i - LAG)

    for j in range(HALF - LAG, HALF):
        share(j)

    def put(out, half, k, x):
        out[:, lanes(half, k)] = x.T

    for j in range(HALF):
        m_back(j).wait_recv()
    for k in range(chunks):
        part = pl.ds(k * LANES, LANES)
        put(dk_out, core, k, own[0, part])
        put(dk_out, other, k, theirs[1, part])
        put(dv_out, core, k, own[1, part])
        put(dv_out, other, k, theirs[2, part])

    for i in range(2):
        x_stat(i).wait_send()
    m_stat().wait_send()

    @pl.loop(0, HALF)
    def _(j):
        x_near(j).wait_send()
        x_cross(j).wait_send()
        m_q(j).wait_send()
        m_k(j).wait_send()
        m_back(j).wait_send()

        @pl.when(has_src)
        def _():
            z_k(0, j).wait_send()
            z_k(1, j).wait_send()

        @pl.when(has_fwd)
        def _():
            z_back(j).wait_send()

    ready = 0
    for k in range(chunks):
        done = -(-(k + 1) * LANES // (dim * PAIR))
        for j in range(ready, done):
            part = rows(j * PAIR, PAIR)
            for i in range(2):
                x_back(i, j).wait_send()
                x_back_in(i, j).wait_recv()
        ready = done
        part = pl.ds(k * LANES, LANES)
        put(dq_out, core, k, (dqo[core, part] * scale + xback[core, part].astype(F32)).astype(BF16))
        put(dq_out, other, k, (theirs[0, part].astype(F32) + xback[other, part].astype(F32)).astype(BF16))


def store(a, b, c, x, y, z, sems):
    copies = [pltpu.make_async_copy(s, d, sems.at[i]) for i, (s, d) in enumerate(((a, x), (b, y), (c, z)))]
    for copy in copies:
        copy.start()
    for copy in copies:
        copy.wait()


def per_device(count, query_rows, key_rows, value_rows, out_rows, grad_out, normalizer, keep_tasks):
    block, width = query_rows.shape
    dim = width // HEADS
    half = width // 2
    vmem = pl.BlockSpec(memory_space=pltpu.VMEM)
    hbm = pl.BlockSpec(memory_space=pl.ANY)
    dma = pltpu.SemaphoreType.DMA
    outs = [jax.ShapeDtypeStruct((block, width), BF16)] * 3
    packed = pl.pallas_call(
        functools.partial(kernel, count),
        out_shape=[pltpu.VMEM((block, width), BF16)] * 3,
        in_specs=[hbm] * 7,
        out_specs=[vmem] * 3,
        scratch_shapes=[
            *[pltpu.VMEM((block, width), BF16)] * 5,
            pltpu.VMEM(normalizer.shape, F32),
            pltpu.SMEM(keep_tasks.shape[::-1], jnp.int32),
            pltpu.VMEM((4, HALF, 2, dim, block), BF16),
            pltpu.VMEM((HALF, 2, dim, block), BF16),
            pltpu.VMEM((4, HALF, 2, dim, block), BF16),
            pltpu.VMEM((HALF, 2, dim, block), BF16),
            pltpu.VMEM((4, 2, HALF, block), F32),
            pltpu.VMEM((2, HALF, block), F32),
            pltpu.VMEM((2, half, block), F32),
            pltpu.VMEM((HALF, 2, 2, dim, block), F32),
            pltpu.VMEM((HALF, 2, 2, dim, block), BF16),
            pltpu.VMEM((HALF, 2, 2, dim, block), BF16),
            *[pltpu.VMEM((2, half, block), BF16)] * 3,
            pltpu.VMEM((3, half, block), BF16),
            pltpu.VMEM((3, half, block), BF16),
            dma((13,)),
            dma((2, HALF)), dma((2, HALF)), dma((2,)), dma((2,)),
            dma((HALF,)), dma((HALF,)), dma((HALF,)), dma((HALF,)), dma, dma,
            dma((2, HALF)), dma((2, HALF)),
            dma((HALF,)), dma((HALF,)),
            dma((2, HALF // PAIR)), dma((2, HALF // PAIR)),
            dma((HALF,)), dma((HALF,)),
        ],
        compiler_params=pltpu.CompilerParams(
            collective_id=0, has_side_effects=True, vmem_limit_bytes=40 * 1024 * 1024
        ),
    )(*[pltpu.with_memory_space_constraint(x, pltpu.HBM) for x in (query_rows, key_rows, value_rows, out_rows, grad_out, normalizer, keep_tasks.T)])
    return pl.pallas_call(
        store,
        out_shape=outs,
        in_specs=[vmem] * 3,
        out_specs=[hbm] * 3,
        scratch_shapes=[dma((3,))],
    )(*[pltpu.with_memory_space_constraint(x, pltpu.VMEM) for x in packed])


def solution(mesh):
    rows = P(("groups", "tok"), None)
    return jax.shard_map(
        functools.partial(per_device, mesh.shape["tok"]),
        mesh=mesh,
        in_specs=(rows,) * 5 + (P(None, ("groups", "tok")), P("groups", None)),
        out_specs=(rows,) * 3,
        check_vma=False,
    )
```

```python
import functools

import jax
import jax.numpy as jnp
from jax import lax
from jax.experimental import pallas as pl
from jax.experimental.pallas import tpu as pltpu
from jax.sharding import PartitionSpec as P

HEADS = 16
HALF = HEADS // 2
LANES = 128
LOG2E = 1.4426950408889634
CENTRE = 4.0
MESH = pl.DeviceIdType.MESH
F32 = jnp.float32
BF16 = jnp.bfloat16
AHEAD = 5
LAG = 3
PAIR = 2


def dot_nn(a, b):
    return lax.dot_general(a, b, (((1,), (0,)), ((), ())), preferred_element_type=F32)


def dot_nt(a, b):
    return lax.dot_general(a, b, (((1,), (1,)), ((), ())), preferred_element_type=F32)


def kernel(
    count, q_hbm, k_hbm, v_hbm, o_hbm, g_hbm, lse_hbm, keep_hbm,
    dq_out, dk_out, dv_out,
    q_in, k_in, v_in, o_in, g_in, lse_ref, keep_ref, lout, lin,
    qbuf, qaway, kbuf, kaway, sbuf, saway, dqo, dkv,
    zout, zback, xout, xback, own, mine, theirs,
    ins, xs, xr, xss, xsr, xls, xlr, ms, mr, ks, kr, mss, msr, zs, zr, bs, br, rs, rr, fs, fr,
):
    tok = lax.axis_index("tok")
    core, chip = tok % 2, tok // 2
    side, plane = chip % 2, chip // 2
    planes = count // 4
    other = 1 - core
    mate = tok + 1 - 2 * core
    across = 2 * (chip + 1 - 2 * side)
    step = 4 * (1 - 2 * side)
    fwd, src = tok + step, tok - step
    has_low, has_high = plane > 0, plane < planes - 1
    has_fwd = jnp.logical_or(jnp.logical_and(side == 0, has_high), jnp.logical_and(side == 1, has_low))
    has_src = jnp.logical_or(jnp.logical_and(side == 0, has_low), jnp.logical_and(side == 1, has_high))
    width = q_in.shape[1]
    dim = width // HEADS
    scale = dim ** -0.5

    barrier = pltpu.get_barrier_semaphore()

    def greet(target):
        pl.semaphore_signal(barrier, inc=1, device_id={"tok": target}, device_id_type=MESH)

    greet(mate)
    greet(across)
    greet(across + 1)

    @pl.when(has_fwd)
    def _():
        greet(fwd)
        greet(fwd + other - core)

    @pl.when(has_src)
    def _():
        greet(src)
        greet(src + other - core)

    half_width = q_in.shape[1] // 2
    loads = []

    def load(src_ref, dst_ref):
        copy = pltpu.make_async_copy(src_ref, dst_ref, ins.at[len(loads)])
        copy.start()
        loads.append(copy)

    for lo, hi in ((0, LANES), (LANES, half_width)):
        for src_ref, dst_ref in ((q_hbm, q_in), (g_hbm, g_in)):
            for base in (0, half_width):
                part = (slice(None), pl.ds(base + lo, hi - lo))
                load(src_ref.at[part], dst_ref.at[part])
    for src_ref, dst_ref in ((o_hbm, o_in), (lse_hbm, lse_ref), (k_hbm, k_in), (v_hbm, v_in), (keep_hbm, keep_ref)):
        load(src_ref, dst_ref)

    def remote(src_ref, dst_ref, send, recv, target):
        return pltpu.make_async_remote_copy(
            src_ref=src_ref, dst_ref=dst_ref, send_sem=send, recv_sem=recv,
            device_id={"tok": target}, device_id_type=MESH,
        )

    def x_near(j):
        return remote(qbuf.at[core, j], qbuf.at[2 + core, j], xs.at[0, j], xr.at[0, j], across + core)

    def x_cross(j):
        return remote(qaway.at[j], qbuf.at[2 + core, j], xs.at[1, j], xr.at[1, j], across + other)

    def x_stat(i):
        return remote(sbuf.at[core, 1] if i == 0 else saway.at[1], sbuf.at[2 + core, 1], xss.at[i], xsr.at[i],
                      across + (core if i == 0 else other))

    def x_lse(i):
        return remote(lout.at[i], lin.at[core], xls.at[i], xlr.at[i], across + (core if i == 0 else other))

    def x_lse_in(i):
        parity = core if i == 0 else other
        return remote(lout.at[0], lin.at[parity], xls.at[i], xlr.at[i], across)

    def x_in(i, j):
        parity = core if i == 0 else other
        return remote(qaway.at[0], qbuf.at[2 + parity, j], xs.at[i, j], xr.at[i, j], across)

    def x_stat_in(i):
        parity = core if i == 0 else other
        return remote(saway.at[1], sbuf.at[2 + parity, 1], xss.at[i], xsr.at[i], across)

    def m_q(j):
        return remote(qaway.at[j], qbuf.at[core, j], ms.at[j], mr.at[j], mate)

    def m_k(j):
        return remote(kaway.at[j], kbuf.at[core, j], ks.at[j], kr.at[j], mate)

    def m_stat():
        return remote(saway, sbuf.at[core], mss, msr, mate)

    def m_q_in(j):
        return remote(qaway.at[0], qbuf.at[other, j], ms.at[j], mr.at[j], mate)

    def m_k_in(j):
        return remote(kaway.at[0], kbuf.at[other, j], ks.at[j], kr.at[j], mate)

    def m_stat_in():
        return remote(saway, sbuf.at[other], mss, msr, mate)

    def z_k(i, j):
        return remote(kbuf.at[core, j] if i == 0 else kaway.at[j], kbuf.at[2 + core, j],
                      zs.at[i, j], zr.at[i, j], src + (0 if i == 0 else other - core))

    def z_k_in(i, j):
        parity = core if i == 0 else other
        return remote(kaway.at[0], kbuf.at[2 + parity, j], zs.at[i, j], zr.at[i, j], fwd)

    def z_back(j):
        return remote(zout.at[j], zback.at[j], bs.at[j], br.at[j], fwd)

    def z_back_in(j):
        return remote(zout.at[j], zback.at[j], bs.at[j], br.at[j], src)

    def rows(j, n=1):
        return pl.ds(pl.multiple_of(j * dim, 16), n * dim)

    def x_back(i, j):
        part = rows(j * PAIR, PAIR)
        to = core if i == 0 else other
        return remote(xout.at[to, part], xback.at[core, part], rs.at[i, j], rr.at[i, j], across + to)

    def x_back_in(i, j):
        part = rows(j * PAIR, PAIR)
        return remote(xout.at[0, part], xback.at[core if i == 0 else other, part], rs.at[i, j], rr.at[i, j], across)

    def m_back(j):
        return remote(mine.at[:, rows(j)], theirs.at[:, rows(j)], fs.at[j], fr.at[j], mate)

    def lanes(half, k):
        return pl.ds(pl.multiple_of(half * half_width + k * LANES, LANES), LANES)

    def pieces(k):
        at = k * LANES
        while at < (k + 1) * LANES:
            j = at // dim
            end = min((j + 1) * dim, (k + 1) * LANES)
            yield j, at - j * dim, end - j * dim, at - k * LANES, end - k * LANES
            at = end

    def flip(ref, k, near, far, i):
        for half, put in ((core, near), (other, far)):
            block = ref[:, lanes(half, k)].T
            for j, lo, hi, a, b in pieces(k):
                put(j, i, lo, hi, block[a:b])

    def q_near(j, i, lo, hi, x):
        qbuf[core, j, i, lo:hi] = x

    def q_far(j, i, lo, hi, x):
        qaway[j, i, lo:hi] = x

    def k_near(j, i, lo, hi, x):
        kbuf[core, j, i, lo:hi] = x

    def k_far(j, i, lo, hi, x):
        kaway[j, i, lo:hi] = x

    chunks = half_width // LANES
    ready = 0
    for k in range(chunks):
        if k == 0:
            for copy in loads[:4]:
                copy.wait()
        flip(q_in, k, q_near, q_far, 0)
        flip(g_in, k, q_near, q_far, 1)
        if k == 0:
            pl.semaphore_wait(barrier, 3 + 2 * has_fwd.astype(jnp.int32) + 2 * has_src.astype(jnp.int32))
        done = (k + 1) * LANES // dim
        for j in range(ready, done):
            x_near(j).start()
            x_cross(j).start()
        for j in range(ready, done):
            m_q(j).start()
        ready = done
        if k == 0:
            for copy in loads[4:10]:
                copy.wait()
            head = lax.broadcasted_iota(jnp.int32, (HEADS, width), 0) * dim
            lane = lax.broadcasted_iota(jnp.int32, (HEADS, width), 1)
            pick = jnp.where(jnp.logical_and(lane >= head, lane < head + dim), 1.0, 0.0).astype(BF16)
            prod = g_in[...].astype(F32) * o_in[...].astype(F32)
            high = prod.astype(BF16)
            low = (prod - high.astype(F32)).astype(BF16)
            delta = dot_nt(pick, high) + dot_nt(pick, low)
            lse = lse_ref[...]
            lse2 = lse * LOG2E
            first = core == 0
            centred = lse - CENTRE
            lout[0] = jnp.where(first, centred[:HALF], centred[HALF:]).astype(BF16)
            lout[1] = jnp.where(first, centred[HALF:], centred[:HALF]).astype(BF16)
            sbuf[core, 0] = jnp.where(first, lse2[:HALF], lse2[HALF:])
            sbuf[core, 1] = jnp.where(first, delta[:HALF], delta[HALF:])
            saway[0] = jnp.where(first, lse2[HALF:], lse2[:HALF])
            saway[1] = jnp.where(first, delta[HALF:], delta[:HALF])
            for i in range(2):
                x_lse(i).start()
                x_stat(i).start()
            m_stat().start()

    for copy in loads[10:]:
        copy.wait()
    ready = 0
    for k in range(chunks):
        flip(k_in, k, k_near, k_far, 0)
        flip(v_in, k, k_near, k_far, 1)
        done = (k + 1) * LANES // dim
        for j in range(ready, done):
            m_k(j).start()

        @pl.when(has_src)
        def _():
            for j in range(ready, done):
                z_k(0, j).start()
                z_k(1, j).start()

        ready = done

    @pl.when(jnp.logical_not(has_src))
    def _():
        zback[...] = jnp.zeros(zback.shape, BF16)

    first_block = plane * 4 + side * 2
    across_block = plane * 4 + (1 - side) * 2

    def task(key, slot, query, j, keys, values):
        flag = keep_ref[key - query + 2, query]
        gone = (1 - flag).astype(F32) * 1e30
        q_t, g_t = qbuf[slot, j, 0], qbuf[slot, j, 1]
        lse = sbuf[slot, 0, pl.ds(j, 1), :] + gone
        delta = sbuf[slot, 1, pl.ds(j, 1), :]
        probs = jnp.exp2(dot_nn(keys, q_t) * (scale * LOG2E) - lse)
        grad = (probs * (dot_nn(values, g_t) - delta)).astype(BF16)
        return q_t, g_t, grad, probs.astype(BF16)

    def run(j, work):
        found, sums = {}, []
        for c, key, slots in work:
            keys_t = kbuf[c, j, 0]
            keys = keys_t.T
            values = kbuf[c, j, 1].T
            parts = [task(key, slot, query, j, keys, values) for slot, query, _ in slots]
            q_all, g_all, grads, lows = [jnp.concatenate([p[i] for p in parts], axis=1) for i in range(4)]
            sums.append((dot_nn(grads, q_all.T).T, dot_nn(lows, g_all.T).T))
            for (_, _, name), p in zip(slots, parts):
                found.setdefault(name, []).append((keys_t, p[2]))
        out = {
            name: dot_nn(
                jnp.concatenate([t[0] for t in terms], axis=1),
                jnp.concatenate([t[1] for t in terms], axis=0),
            )
            for name, terms in found.items()
        }
        return out, sums

    def inner(j):
        m_q_in(j).wait_recv()
        m_k_in(j).wait_recv()

        @pl.when(j == 0)
        def _():
            m_stat_in().wait_recv()

        queries = [(b, first_block + b, b) for b in range(2)]
        got, sums = run(j, [(c, first_block + c, queries) for c in range(2)])
        for b in range(2):
            dqo[b, rows(j)] = got[b]
            dkv[j, b, 0] = sums[b][0]
            dkv[j, b, 1] = sums[b][1]

    near = (2 + side, across_block + side, 0)
    far = (3 - side, across_block + 1 - side, 1)
    close = 1 - side
    local = [(close, first_block + close, [near, far]), (1 - close, first_block + 1 - close, [near])]
    beyond = [(2 + side, first_block + step + side, [near, far]), (3 - side, first_block + step + 1 - side, [far])]

    def x_run(j):
        x_in(0, j).wait_recv()
        x_in(1, j).wait_recv()

        @pl.when(j == 0)
        def _():
            for i in range(2):
                x_lse_in(i).wait_recv()
                x_stat_in(i).wait_recv()
            for b in range(2):
                sbuf[2 + b, 0] = (lin[b].astype(F32) + CENTRE) * LOG2E

        def finish(got, sums):
            for i, c in enumerate((close, 1 - close)):
                dkv[j, c, 0] += sums[i][0]
                dkv[j, c, 1] += sums[i][1]
            xout[side, rows(j)] = (got[0] * scale).astype(BF16)
            xout[1 - side, rows(j)] = (got[1] * scale).astype(BF16)

        @pl.when(has_fwd)
        def _():
            z_k_in(0, j).wait_recv()
            z_k_in(1, j).wait_recv()
            got, sums = run(j, local + beyond)
            finish(got, sums[:2])
            for i, c in enumerate((side, 1 - side)):
                zout[j, c, 0] = (sums[2 + i][0] * scale).astype(BF16)
                zout[j, c, 1] = sums[2 + i][1].astype(BF16)
        @pl.when(jnp.logical_not(has_fwd))
        def _():
            finish(*run(j, local))

        @pl.when(j % PAIR == PAIR - 1)
        def _():
            x_back(0, j // PAIR).start()
            x_back(1, j // PAIR).start()

        @pl.when(has_fwd)
        def _():
            z_back(j).start()

    def share(j):
        @pl.when(has_src)
        def _():
            z_back_in(j).wait_recv()

        def total(c):
            return ((dkv[j, c, 0] * scale + zback[j, c, 0].astype(F32)).astype(BF16),
                    (dkv[j, c, 1] + zback[j, c, 1].astype(F32)).astype(BF16))

        mine[0, rows(j)] = (dqo[other, rows(j)] * scale).astype(BF16)
        mine[1, rows(j)], mine[2, rows(j)] = total(other)
        m_back(j).start()
        own[0, rows(j)], own[1, rows(j)] = total(core)

    for j in range(AHEAD):
        inner(j)

    @pl.loop(0, HALF)
    def _(i):
        x_run(i)

        @pl.when(i + AHEAD < HALF)
        def _():
            inner(i + AHEAD)

        @pl.when(i >= LAG)
        def _():
            share(i - LAG)

    for j in range(HALF - LAG, HALF):
        share(j)

    def put(out, half, k, x):
        out[:, lanes(half, k)] = x.T

    for j in range(HALF):
        m_back(j).wait_recv()
    for k in range(chunks):
        part = pl.ds(k * LANES, LANES)
        put(dk_out, core, k, own[0, part])
        put(dk_out, other, k, theirs[1, part])
        put(dv_out, core, k, own[1, part])
        put(dv_out, other, k, theirs[2, part])

    for i in range(2):
        x_stat(i).wait_send()
        x_lse(i).wait_send()
    m_stat().wait_send()

    @pl.loop(0, HALF)
    def _(j):
        x_near(j).wait_send()
        x_cross(j).wait_send()
        m_q(j).wait_send()
        m_k(j).wait_send()
        m_back(j).wait_send()

        @pl.when(has_src)
        def _():
            z_k(0, j).wait_send()
            z_k(1, j).wait_send()

        @pl.when(has_fwd)
        def _():
            z_back(j).wait_send()

    ready = 0
    for k in range(chunks):
        done = -(-(k + 1) * LANES // (dim * PAIR))
        part = pl.ds(k * LANES, LANES)
        for i in range(2):
            for j in range(ready, done):
                x_back(i, j).wait_send()
                x_back_in(i, j).wait_recv()
            if i == 0:
                total = dqo[core, part] * scale + xback[core, part].astype(F32)
                put(dq_out, core, k, total.astype(BF16))
            else:
                total = theirs[0, part].astype(F32) + xback[other, part].astype(F32)
                put(dq_out, other, k, total.astype(BF16))
        ready = done


def store(a, b, c, x, y, z, sems):
    copies = [pltpu.make_async_copy(s, d, sems.at[i]) for i, (s, d) in enumerate(((a, x), (b, y), (c, z)))]
    for copy in copies:
        copy.start()
    for copy in copies:
        copy.wait()


def per_device(count, query_rows, key_rows, value_rows, out_rows, grad_out, normalizer, keep_tasks):
    block, width = query_rows.shape
    dim = width // HEADS
    half = width // 2
    vmem = pl.BlockSpec(memory_space=pltpu.VMEM)
    hbm = pl.BlockSpec(memory_space=pl.ANY)
    dma = pltpu.SemaphoreType.DMA
    outs = [jax.ShapeDtypeStruct((block, width), BF16)] * 3
    packed = pl.pallas_call(
        functools.partial(kernel, count),
        out_shape=[pltpu.VMEM((block, width), BF16)] * 3,
        in_specs=[hbm] * 7,
        out_specs=[vmem] * 3,
        scratch_shapes=[
            *[pltpu.VMEM((block, width), BF16)] * 5,
            pltpu.VMEM(normalizer.shape, F32),
            pltpu.SMEM(keep_tasks.shape[::-1], jnp.int32),
            pltpu.VMEM((2, HALF, block), BF16),
            pltpu.VMEM((2, HALF, block), BF16),
            pltpu.VMEM((4, HALF, 2, dim, block), BF16),
            pltpu.VMEM((HALF, 2, dim, block), BF16),
            pltpu.VMEM((4, HALF, 2, dim, block), BF16),
            pltpu.VMEM((HALF, 2, dim, block), BF16),
            pltpu.VMEM((4, 2, HALF, block), F32),
            pltpu.VMEM((2, HALF, block), F32),
            pltpu.VMEM((2, half, block), F32),
            pltpu.VMEM((HALF, 2, 2, dim, block), F32),
            pltpu.VMEM((HALF, 2, 2, dim, block), BF16),
            pltpu.VMEM((HALF, 2, 2, dim, block), BF16),
            *[pltpu.VMEM((2, half, block), BF16)] * 3,
            pltpu.VMEM((3, half, block), BF16),
            pltpu.VMEM((3, half, block), BF16),
            dma((13,)),
            dma((2, HALF)), dma((2, HALF)), dma((2,)), dma((2,)), dma((2,)), dma((2,)),
            dma((HALF,)), dma((HALF,)), dma((HALF,)), dma((HALF,)), dma, dma,
            dma((2, HALF)), dma((2, HALF)),
            dma((HALF,)), dma((HALF,)),
            dma((2, HALF // PAIR)), dma((2, HALF // PAIR)),
            dma((HALF,)), dma((HALF,)),
        ],
        compiler_params=pltpu.CompilerParams(
            collective_id=0, has_side_effects=True, vmem_limit_bytes=40 * 1024 * 1024
        ),
    )(*[pltpu.with_memory_space_constraint(x, pltpu.HBM) for x in (query_rows, key_rows, value_rows, out_rows, grad_out, normalizer, keep_tasks.T)])
    return pl.pallas_call(
        store,
        out_shape=outs,
        in_specs=[vmem] * 3,
        out_specs=[hbm] * 3,
        scratch_shapes=[dma((3,))],
    )(*[pltpu.with_memory_space_constraint(x, pltpu.VMEM) for x in packed])


def solution(mesh):
    rows = P(("groups", "tok"), None)
    return jax.shard_map(
        functools.partial(per_device, mesh.shape["tok"]),
        mesh=mesh,
        in_specs=(rows,) * 5 + (P(None, ("groups", "tok")), P("groups", None)),
        out_specs=(rows,) * 3,
        check_vma=False,
    )
```
